32 devices in a mesh: row: 8 (over y, x, core), col: 4 (over z).
Axes of the slice: x: 2, y: 2, z: 4, core: 2. Of those that a mesh axis runs over, the one named last changes fastest.
Arguments:
- chol: bfloat16 [3, 6144, 2048], P(None, 'row', 'col'), may hold values from -0.67578125 to 0.67578125
- amps: bfloat16 [9, 2048, 2048], P(None, 'row', 'col'), may hold values from -0.19921875 to 0.19921875
- eps_occ: float32 [3], replicated, may hold values from -2 to -0.5
- eps_vir: float32 [2048], replicated, may hold values from 1 to 8
- pairs: int32 [9, 2], replicated, may hold values from 0 to 2, as said below
Outputs:
- residual: float32 [9, 2048, 2048], P(None, 'row', 'col')
The draws below stay inside these ranges and needn't reach their ends.
Inputs may be any that keep to these rules, and one draw needn't show every extreme that they name: `pairs`: the rows list every ordered pair (i, j) of orbitals 0 to 2 exactly once.
All inputs are finite; a program needn't handle non-finite values.
Results may differ from the reference program's by a relative error of at most 0.0039.
Values may be sent and summed in bfloat16 or wider, within the bound.
A program may use at most 128 MiB of HBM per device.

```python
import jax
import jax.numpy as jnp

NVIR = 2048
NCHOL = 6144
OCC = 3
SLABS = 9


def draw_pairs(key, part):
    order = jax.random.permutation(jax.random.fold_in(key, 17), OCC * OCC).astype(jnp.int32)
    return jnp.stack([order // OCC, order % OCC], axis=1).astype(jnp.int32)


def level_of(rng, extent, shards, least, high):
    factor_of, own = 1.0, jax.random.fold_in(rng, 6)
    for dim, shards_of in shards:
        steps = jnp.exp(jax.random.uniform(jax.random.fold_in(own, dim), (shards_of,), jnp.float32, least / len(shards), high / len(shards)))
        factor_of = factor_of * jnp.repeat(steps, extent[dim] // shards_of).reshape([-1 if axis == dim else 1 for axis in range(len(extent))])
    return factor_of


def noise(key, shape, width, bound, shards=(), kind=jnp.bfloat16):
    gain = level_of(key, shape, shards, -0.22, 0.18) if shards else 1.0
    drawn = jax.random.normal(key, shape, jnp.float32) * width * gain
    return jnp.minimum(jnp.maximum(drawn, -bound), bound).astype(kind)


def setup_inputs(seed: int = 0) -> dict:
    arg_keys = jax.random.split(jax.random.key(seed), 6)
    return {
        "chol": noise(arg_keys[0], (OCC, NCHOL, NVIR), (NCHOL ** -0.25), 0.67578125, ((1, 8), (2, 4))),
        "amps": noise(arg_keys[1], (SLABS, NVIR, NVIR), 0.03, 0.19921875, ((1, 8), (2, 4))),
        "eps_occ": jnp.clip(jax.random.uniform(arg_keys[2], (OCC,), jnp.float32, -2.0, -0.5), -2.0, -0.5),
        "eps_vir": jnp.clip(jax.random.uniform(arg_keys[3], (NVIR,), jnp.float32, 1.0, 8.0), 1.0, 8.0),
        "pairs": draw_pairs(jax.random.fold_in(arg_keys[5], 71), 0),
    }


def tdot(left, right):
    return jnp.dot(left.T, right, preferred_element_type=jnp.float32)


def reference(chol, amps, eps_occ, eps_vir, pairs):
    order = jnp.arange(SLABS, dtype=jnp.int32)
    slot = jnp.zeros((OCC, OCC), jnp.int32).at[pairs[:, 0], pairs[:, 1]].set(order)
    amp = [[amps[slot[k, l]] for l in range(OCC)] for k in range(OCC)]
    coulomb = [[tdot(chol[k], chol[l]) for l in range(OCC)] for k in range(OCC)]
    coulomb_b = [[block.astype(jnp.bfloat16) for block in line] for line in coulomb]
    dressed = []
    for k in range(OCC):
        line = []
        for j in range(OCC):
            total = coulomb[k][j]
            for l in range(OCC):
                total = total + jnp.dot(coulomb_b[k][l], amp[l][j], preferred_element_type=jnp.float32)
            line.append(total)
        dressed.append(line)
    dressed_b = [[block.astype(jnp.bfloat16) for block in line] for line in dressed]
    results = []
    for i in range(OCC):
        for j in range(OCC):
            denom = eps_vir[:, None] + eps_vir[None, :] - eps_occ[i] - eps_occ[j]
            result = denom * amp[i][j].astype(jnp.float32) + dressed[i][j]
            for k in range(OCC):
                result = result + jnp.dot(amp[i][k], dressed_b[k][j], preferred_element_type=jnp.float32)
            results.append(result)
    stacked = jnp.stack(results, axis=0)
    flat_pair = (pairs[:, 0] * OCC + pairs[:, 1]).astype(jnp.int32)
    return jnp.take(stacked, flat_pair, axis=0)
```

```python
import functools

import jax
import jax.numpy as jnp
from jax import lax
from jax.experimental import pallas as pl
from jax.experimental.pallas import tpu as pltpu
from jax.sharding import PartitionSpec as P

F32 = jnp.float32
BF16 = jnp.bfloat16
MESH = pl.DeviceIdType.MESH
PLANE = 8
CHAIN = 4
PIECES = 11


def remote(src, dst, send, recv, where):
    return pltpu.make_async_remote_copy(
        src_ref=src, dst_ref=dst, send_sem=send, recv_sem=recv, device_id=where, device_id_type=MESH
    )


def times(left, right):
    return jnp.dot(left, right, preferred_element_type=F32)


class Gather:
    def __init__(self, view, own, size, send, recv):
        me = lax.axis_index("row")
        core, xbit, ybit = lax.rem(me, 2), lax.rem(me // 2, 2), me // 4
        sib, xn, yn = me + 1 - 2 * core, me + 2 - 4 * xbit, me + 4 - 8 * ybit
        far = xn + 4 - 8 * ybit
        half = size // 2

        def part(origin, low, count):
            return view(pl.multiple_of(origin * size + low, 16), count)

        def make(index, src, dst, where):
            return remote(src, dst, send.at[index], recv.at[index], {"row": where})

        def hand_on(index, origin, low, count, where):
            return make(index, part(origin, low, count), part(origin, low, count), where)

        self.copies = [
            make(0, own(0, half), part(me, 0, half), xn),
            make(1, own(half, half), part(me, half, half), xn),
            make(2, own(half, half), part(me, half, half), yn),
            make(3, own(0, half), part(me, 0, half), yn),
            make(4, own(0, size), part(me, 0, size), sib),
            hand_on(5, xn, 0, half, yn),
            hand_on(6, yn, half, half, xn),
            hand_on(7, xn, 0, size, sib),
            hand_on(8, yn, 0, size, sib),
            hand_on(9, far, 0, half, sib),
            hand_on(10, far, half, half, sib),
        ]

    def begin(self):
        for index in (0, 2, 1, 3, 4):
            self.copies[index].start()

    def relay(self):
        for arrived, onward in ((0, 5), (2, 6), (1, 7), (3, 8)):
            self.copies[arrived].wait_recv()
            self.copies[onward].start()

    def last(self):
        for arrived, onward in ((5, 9), (6, 10)):
            self.copies[arrived].wait_recv()
            self.copies[onward].start()

    def arrived(self):
        for index in (4, 7, 8, 9, 10):
            self.copies[index].wait_recv()

    def sent(self):
        for copy in self.copies:
            copy.wait_send()


class Chain:
    def __init__(self, panel, own, count, send, recv):
        self.panel, self.own, self.count, self.send, self.recv = panel, own, count, send, recv
        self.z = lax.axis_index("col")

    def origin(self, way, dist):
        return self.z + dist * (1 - 2 * way)

    def exists(self, way, dist):
        origin = self.origin(way, dist)
        return jnp.logical_and(origin >= 0, origin < CHAIN)

    def onward(self, way):
        return self.exists(1 - way, 1)

    def hop(self, way, dist, k, own=False):
        origin = self.z if own else self.origin(way, dist - 1)
        src = self.own.at[k] if own else self.panel.at[origin, k]
        where = {"col": self.z - 1 + 2 * way}
        return remote(
            src, self.panel.at[origin, k], self.send.at[way, dist - 1, k], self.recv.at[way, dist - 1, k], where
        )

    def begin(self, way):
        @pl.when(self.onward(way))
        def _():
            for k in range(self.count):
                self.hop(way, 1, k, own=True).start()

    def arrive(self, way, dist, k):
        origin = self.origin(way, dist)
        sem = (way, dist - 1, k)
        remote(
            self.panel.at[origin, k], self.panel.at[origin, k], self.send.at[sem], self.recv.at[sem],
            {"col": origin},
        ).wait_recv()

        @pl.when(self.onward(way))
        def _():
            self.hop(way, dist + 1, k).start()

    def sent(self, way):
        for dist in range(1, CHAIN):
            @pl.when(jnp.logical_and(self.onward(way), self.exists(way, dist - 1)))
            def _():
                for k in range(self.count):
                    self.hop(way, dist, k, own=dist == 1).wait_send()


def whole_kernel(
    chol_ref, slabs_ref, left_ref, r_ref, tr_ref,
    cp, tc, ct, cts, yb, acc, ss1, rr1, ss2, rr2,
    local, cz_s, cz_r, tz_s, tz_r, ag_s, ag_r, ct_s, ct_r, y_s, y_r, rs1_s, rs1_r, rs2_s, rs2_r,
):
    occ, depth, wide = chol_ref.shape
    size = slabs_ref.shape[2]
    tall = occ * size
    half = wide // 2
    me, z = lax.axis_index("row"), lax.axis_index("col")
    core, chip = lax.rem(me, 2), me // 2
    xbit, ybit = lax.rem(chip, 2), chip // 2
    sib, xn, yn = me + 1 - 2 * core, me + 2 - 4 * xbit, me + 4 - 8 * ybit
    inner = jnp.logical_and(z > 0, z < CHAIN - 1)
    centre = 1 - (2 * z) // CHAIN

    def along(first):
        return xn + first * (yn - xn)

    barrier = pltpu.get_barrier_semaphore()

    def greet(where):
        pl.semaphore_signal(barrier, inc=1, device_id=where, device_id_type=MESH)

    for row in (sib, xn, yn):
        greet({"row": row})

    @pl.when(z > 0)
    def _():
        greet({"col": z - 1})

    @pl.when(z < CHAIN - 1)
    def _():
        greet({"col": z + 1})

    @pl.when(inner)
    def _():
        pl.semaphore_wait(barrier, 5)

    @pl.when(jnp.logical_not(inner))
    def _():
        pl.semaphore_wait(barrier, 4)

    chols = Chain(cp, chol_ref, occ, cz_s, cz_r)
    amps = Chain(tr_ref, left_ref, occ, tz_s, tz_r)
    cols = Gather(
        lambda low, count: tc.at[:, :, pl.ds(low, count), :],
        lambda low, count: slabs_ref.at[:, :, pl.ds(low, count), :],
        size, ag_s.at[occ], ag_r.at[occ],
    )
    chols.begin(0)
    chols.begin(1)
    cols.begin()
    keep_c = pltpu.make_async_copy(chol_ref, cp.at[z], local.at[0])
    keep_t = pltpu.make_async_copy(
        slabs_ref, tc.at[:, :, pl.ds(pl.multiple_of(me * size, size), size), :], local.at[1]
    )
    keep_c.start()
    keep_t.start()
    keep_c.wait()
    keep_t.wait()

    def near(k, carry):
        for way in (0, 1):
            @pl.when(chols.exists(way, 1))
            def _():
                chols.arrive(way, 1, k)
        return carry

    lax.fori_loop(0, occ, near, 0)
    cols.relay()

    def first_y(j, carry):
        acc[j] = cp[z, j].astype(F32)
        return carry

    lax.fori_loop(0, occ, first_y, 0)
    cols.last()
    cols.arrived()
    cols.sent()

    @pl.when(jnp.logical_not(inner))
    def _():
        chols.sent(centre)
        amps.begin(centre)

    def turned(o, k):
        return remote(
            cts.at[k], ct.at[o, core, pl.ds(pl.multiple_of(k * size, size), size), :],
            ct_s.at[k], ct_r.at[o, k], {"row": sib},
        )

    def use(o, k):
        def half_of(which):
            block = cp[o, k, :, pl.ds(pl.multiple_of(which * size, size), size)]
            return jnp.transpose(block, (1, 0))

        cts[k] = half_of(1 - core)
        turned(o, k).start()
        ct[o, core, pl.ds(pl.multiple_of(k * size, size), size), :] = half_of(core)

        def one(j, carry):
            acc[j] += times(cp[o, k], tc[k, j, pl.ds(pl.multiple_of(o * wide, wide), wide), :])
            return carry

        lax.fori_loop(0, occ, one, 0)

    def come(event, waiting):
        dist, way = (event + 1) // 2, lax.rem(event + 1, 2)
        origin = chols.origin(way, dist)

        @pl.when(chols.exists(way, dist))
        def _():
            def step(k, carry):
                if waiting:
                    chols.arrive(way, dist, k)

                @pl.when(event > 0)
                def _():
                    turned(origin, k).wait_send()

                use(origin, k)
                return carry

            lax.fori_loop(0, occ, step, 0)

    def here(event, carry):
        come(event, False)
        return carry

    def later(event, carry):
        come(event, True)
        return carry

    lax.fori_loop(0, 3, here, 0)
    lax.fori_loop(3, 2 * CHAIN - 1, later, 0)

    @pl.when(inner)
    def _():
        chols.sent(centre)
        amps.begin(centre)

    def y_copy(j):
        mine = yb.at[j, pl.ds(pl.multiple_of(core * depth, depth), depth), :]
        return remote(mine, mine, y_s.at[j], y_r.at[j], {"row": sib})

    def round_y(j, carry):
        yb[j, pl.ds(pl.multiple_of(core * depth, depth), depth), :] = acc[j].astype(BF16)
        y_copy(j).start()
        return carry

    lax.fori_loop(0, occ, round_y, 0)

    def turned_done(k, carry):
        turned(z, k).wait_send()
        for o in range(CHAIN):
            turned(o, k).wait_recv()
        return carry

    lax.fori_loop(0, occ, turned_done, 0)

    def side(first):
        return pl.ds(pl.multiple_of(first * half, half), half)

    def partial(q, j, first):
        return times(ct[q, 0], yb[j, :depth, side(first)]) + times(ct[q, 1], yb[j, depth:, side(first)])

    def rs1(first, j):
        return remote(
            ss1.at[first, j % 2], rr1.at[first, j], rs1_s.at[first, j], rs1_r.at[first, j],
            {"row": along(first)},
        )

    def rs2(first, j):
        return remote(
            ss2.at[first, j % 2], rr2.at[first, j], rs2_s.at[first, j], rs2_r.at[first, j],
            {"row": along(1 - first)},
        )

    def scatter_one(j):
        y_copy(j).wait_recv()
        for first in (0, 1):
            if j > 1:
                rs1(first, j - 2).wait_send()

            def each(n, carry):
                q = (2 * n + 1 - xbit) if first == 0 else (2 * (1 - ybit) + n)
                ss1[first, j % 2, n] = partial(q, j, first).astype(BF16)
                return carry

            lax.fori_loop(0, 2, each, 0)
            rs1(first, j).start()

    def scatter_two(j):
        if j > 1:
            for first in (0, 1):
                rs2(first, j - 2).wait_send()

        def each(first, carry):
            rs1(first, j).wait_recv()
            other = (1 - ybit) + first * (ybit - xbit)
            block = partial(along(1 - first) // 2, j, first) + rr1[first, j, other].astype(F32)
            ss2[first, j % 2] = block.astype(BF16)
            rs2(first, j).start()
            return carry

        lax.fori_loop(0, 2, each, 0)

    def scatter_end(j):
        def each(first, carry):
            mine = ybit + first * (xbit - ybit)
            block = partial(chip, j, first) + rr1[first, j, mine].astype(F32)
            rs2(first, j).wait_recv()
            block += rr2[first, j].astype(F32)
            acc[j, :, side(first)] = block
            for k in range(occ):
                tc[k, j, pl.ds(pl.multiple_of(me * size, size), size), side(first)] = (
                    block[k * size:(k + 1) * size].astype(BF16)
                )
            return carry

        lax.fori_loop(0, 2, each, 0)

    def gather_of(j):
        def view(low, count):
            return tc.at[:, j, pl.ds(low, count), :]

        return Gather(view, lambda low, count: view(pl.multiple_of(me * size + low, 16), count), size, ag_s.at[j], ag_r.at[j])

    gathers = [gather_of(j) for j in range(occ)]

    def bring(dist, own=False):
        if own:
            copy = pltpu.make_async_copy(left_ref, cp.at[z], local.at[0])
            copy.start()
            copy.wait()
            return
        for way in (0, 1):
            @pl.when(amps.exists(way, dist))
            def _():
                def step(k, carry):
                    amps.arrive(way, dist, k)
                    return carry

                lax.fori_loop(0, occ, step, 0)
                origin = amps.origin(way, dist)
                copy = pltpu.make_async_copy(tr_ref.at[origin], cp.at[origin], local.at[0])
                copy.start()
                copy.wait()

    def product(low, high, first, last):
        def each(event, carry):
            dist, way = (event + 1) // 2, lax.rem(event + 1, 2)
            origin = chols.origin(way, dist)

            @pl.when(chols.exists(way, dist))
            def _():
                def step(n, inside):
                    j, k = first + n // occ, lax.rem(n, occ)
                    left = cp[origin, :, pl.ds(pl.multiple_of(k * size, size), size), :].reshape(tall, wide)
                    acc[j] += times(left, tc[k, j, pl.ds(pl.multiple_of(origin * wide, wide), wide), :])
                    return inside

                lax.fori_loop(0, (last - first) * occ, step, 0)

            return carry

        lax.fori_loop(low, high, each, 0)

    scatter_one(0)
    scatter_one(1)
    scatter_two(0)
    scatter_one(2)
    scatter_two(1)
    scatter_end(0)
    gathers[0].begin()
    chols.sent(1 - centre)

    @pl.when(inner)
    def _():
        amps.begin(1 - centre)

    scatter_two(2)
    scatter_end(1)
    gathers[1].begin()
    bring(0, own=True)
    gathers[0].relay()
    scatter_end(2)
    gathers[2].begin()
    bring(1)
    gathers[1].relay()
    gathers[0].last()
    gathers[0].arrived()
    product(0, 3, 0, 1)
    bring(2)
    gathers[2].relay()
    gathers[1].last()
    gathers[1].arrived()
    product(0, 3, 1, 2)
    product(3, 5, 0, 2)
    gathers[2].last()
    gathers[2].arrived()
    product(0, 5, 2, 3)
    bring(3)
    product(5, 7, 0, 3)
    out = pltpu.make_async_copy(acc, r_ref, local.at[0])
    out.start()
    for j in range(occ):
        gathers[j].sent()
    for first in (0, 1):
        for j in (1, 2):
            rs1(first, j).wait_send()
            rs2(first, j).wait_send()

    def y_done(j, carry):
        y_copy(j).wait_send()
        return carry

    lax.fori_loop(0, occ, y_done, 0)
    amps.sent(0)
    amps.sent(1)
    out.wait()


def in_one_kernel(chol, grid):
    occ, depth, wide = chol.shape
    _, size, _ = grid.shape
    tall, full = occ * size, size * PLANE
    slabs = grid.reshape(occ, occ, size, wide)
    left = grid.reshape(occ, tall, wide)
    half = wide // 2
    dma = pltpu.SemaphoreType.DMA
    result, _ = pl.pallas_call(
        whole_kernel,
        out_shape=(
            jax.ShapeDtypeStruct((occ, tall, wide), F32),
            jax.ShapeDtypeStruct((CHAIN, occ, tall, wide), BF16),
        ),
        in_specs=[pl.BlockSpec(memory_space=pl.ANY)] * 3,
        out_specs=(pl.BlockSpec(memory_space=pl.ANY), pl.BlockSpec(memory_space=pl.ANY)),
        scratch_shapes=[
            pltpu.VMEM((CHAIN, occ, depth, wide), BF16),
            pltpu.VMEM((occ, occ, full, wide), BF16),
            pltpu.VMEM((CHAIN, 2, tall, depth), BF16),
            pltpu.VMEM((occ, size, depth), BF16),
            pltpu.VMEM((occ, 2 * depth, wide), BF16),
            pltpu.VMEM((occ, tall, wide), F32),
            pltpu.VMEM((2, 2, 2, tall, half), BF16),
            pltpu.VMEM((2, occ, 2, tall, half), BF16),
            pltpu.VMEM((2, 2, tall, half), BF16),
            pltpu.VMEM((2, occ, tall, half), BF16),
            dma((2,)),
            dma((2, CHAIN - 1, occ)),
            dma((2, CHAIN - 1, occ)),
            dma((2, CHAIN - 1, occ)),
            dma((2, CHAIN - 1, occ)),
            dma((occ + 1, PIECES)),
            dma((occ + 1, PIECES)),
            dma((occ,)),
            dma((CHAIN, occ)),
            dma((occ,)),
            dma((occ,)),
            dma((2, occ)),
            dma((2, occ)),
            dma((2, occ)),
            dma((2, occ)),
        ],
        compiler_params=pltpu.CompilerParams(
            collective_id=0, has_side_effects=True, vmem_limit_bytes=62 * 1024 * 1024
        ),
        cost_estimate=pl.CostEstimate(
            flops=6 * occ * depth * occ * full * wide, bytes_accessed=32 * chol.size, transcendentals=0
        ),
        name="whole",
    )(chol, slabs, left)
    return result.reshape(occ, occ, size, wide)


def in_steps(chol, grid):
    occ, depth, _ = chol.shape
    _, size, wide = grid.shape
    slabs = grid.reshape(occ, occ, size, wide)
    cols = lax.all_gather(slabs, "row", axis=2, tiled=True)
    chol_rows = lax.all_gather(chol, "col", axis=2, tiled=True)
    y = lax.dot_general(chol_rows, cols, (((0, 2), (0, 2)), ((), ())), preferred_element_type=F32)
    y = (y + jnp.transpose(chol, (1, 0, 2)).astype(F32)).astype(BF16)
    swapped = lax.all_to_all(chol_rows, "row", split_axis=2, concat_axis=1, tiled=True)
    y = lax.all_gather(y.reshape(depth, occ * wide), "row", axis=0, tiled=True)
    dressed = lax.dot_general(swapped, y, (((1,), (0,)), ((), ())), preferred_element_type=F32)
    dressed_cols = lax.all_gather(dressed.astype(BF16), "row", axis=1, tiled=True)
    rows = lax.all_gather(slabs, "col", axis=3, tiled=True)
    total = lax.dot_general(rows, dressed_cols, (((1, 3), (0, 1)), ((), ())), preferred_element_type=F32)
    total = (total + dressed).reshape(occ, size, occ, wide)
    return jnp.transpose(total, (2, 0, 1, 3))


def per_device(chol, amps, eps_occ, eps_vir, pairs):
    row_index = lax.axis_index("row")
    col_index = lax.axis_index("col")
    occ = chol.shape[0]
    slabs, size, wide = amps.shape
    order = jnp.arange(slabs, dtype=jnp.int32)
    flat_pair = pairs[:, 0] * occ + pairs[:, 1]
    matches = (flat_pair[None, :] == order[:, None]).astype(jnp.int32)
    slot = jnp.sum(matches * order[None, :], axis=1)
    grid = jnp.take(amps, slot, axis=0, mode="clip")
    one = lax.axis_size("row") == PLANE and lax.axis_size("col") == CHAIN
    product = in_one_kernel(chol, grid) if one else in_steps(chol, grid)
    product = product.reshape(slabs, size, wide)
    product = jnp.take(product, pairs[:, 1] * occ + pairs[:, 0], axis=0, mode="clip")
    rows = lax.dynamic_slice_in_dim(eps_vir, row_index * size, size, 0)
    cols = lax.dynamic_slice_in_dim(eps_vir, col_index * wide, wide, 0)
    high = rows[None, :] - eps_occ[pairs[:, 0]][:, None]
    low = cols[None, :] - eps_occ[pairs[:, 1]][:, None]
    return product + (high[:, :, None] + low[:, None, :]) * amps.astype(F32)


def solution(mesh):
    placed = (P(None, "row", "col"), P(None, "row", "col"), P(), P(), P())
    return jax.shard_map(
        per_device, mesh=mesh, in_specs=placed, out_specs=P(None, "row", "col"), check_vma=False
    )
```

```python
import functools

import jax
import jax.numpy as jnp
from jax import lax
from jax.experimental import pallas as pl
from jax.experimental.pallas import tpu as pltpu
from jax.sharding import PartitionSpec as P

F32 = jnp.float32
BF16 = jnp.bfloat16
MESH = pl.DeviceIdType.MESH
PLANE = 8
CHAIN = 4
PIECES = 11


def remote(src, dst, send, recv, where):
    return pltpu.make_async_remote_copy(
        src_ref=src, dst_ref=dst, send_sem=send, recv_sem=recv, device_id=where, device_id_type=MESH
    )


def times(left, right):
    return jnp.dot(left, right, preferred_element_type=F32)


class Gather:
    def __init__(self, view, own, size, send, recv):
        me = lax.axis_index("row")
        core, xbit, ybit = lax.rem(me, 2), lax.rem(me // 2, 2), me // 4
        sib, xn, yn = me + 1 - 2 * core, me + 2 - 4 * xbit, me + 4 - 8 * ybit
        far = xn + 4 - 8 * ybit
        half = size // 2

        def part(origin, low, count):
            return view(pl.multiple_of(origin * size + low, 16), count)

        def make(index, src, dst, where):
            return remote(src, dst, send.at[index], recv.at[index], {"row": where})

        def hand_on(index, origin, low, count, where):
            return make(index, part(origin, low, count), part(origin, low, count), where)

        self.copies = [
            make(0, own(0, half), part(me, 0, half), xn),
            make(1, own(half, half), part(me, half, half), xn),
            make(2, own(half, half), part(me, half, half), yn),
            make(3, own(0, half), part(me, 0, half), yn),
            make(4, own(0, size), part(me, 0, size), sib),
            hand_on(5, xn, 0, half, yn),
            hand_on(6, yn, half, half, xn),
            hand_on(7, xn, 0, size, sib),
            hand_on(8, yn, 0, size, sib),
            hand_on(9, far, 0, half, sib),
            hand_on(10, far, half, half, sib),
        ]

    def begin(self):
        for index in (0, 2, 1, 3, 4):
            self.copies[index].start()

    def relay(self):
        for arrived, onward in ((0, 5), (2, 6), (1, 7), (3, 8)):
            self.copies[arrived].wait_recv()
            self.copies[onward].start()

    def last(self):
        for arrived, onward in ((5, 9), (6, 10)):
            self.copies[arrived].wait_recv()
            self.copies[onward].start()

    def near(self):
        for index in (4, 7, 8):
            self.copies[index].wait_recv()

    def distant(self):
        for index in (9, 10):
            self.copies[index].wait_recv()

    def sent(self):
        for copy in self.copies:
            copy.wait_send()


class Chain:
    def __init__(self, panel, own, count, send, recv):
        self.panel, self.own, self.count, self.send, self.recv = panel, own, count, send, recv
        self.z = lax.axis_index("col")

    def piece(self, k):
        return pl.ds(k * self.count, self.count)

    def origin(self, way, dist):
        return self.z + dist * (1 - 2 * way)

    def exists(self, way, dist):
        origin = self.origin(way, dist)
        return jnp.logical_and(origin >= 0, origin < CHAIN)

    def onward(self, way):
        return self.exists(1 - way, 1)

    def hop(self, way, dist, k, own=False):
        origin = self.z if own else self.origin(way, dist - 1)
        src = self.own.at[self.piece(k)] if own else self.panel.at[origin, self.piece(k)]
        where = {"col": self.z - 1 + 2 * way}
        return remote(
            src, self.panel.at[origin, self.piece(k)], self.send.at[way, dist - 1, k], self.recv.at[way, dist - 1, k], where
        )

    def begin(self, way):
        @pl.when(self.onward(way))
        def _():
            for k in range(self.count):
                self.hop(way, 1, k, own=True).start()

    def arrive(self, way, dist, k):
        origin = self.origin(way, dist)
        sem = (way, dist - 1, k)
        remote(
            self.panel.at[origin, self.piece(k)], self.panel.at[origin, self.piece(k)],
            self.send.at[sem], self.recv.at[sem], {"col": origin},
        ).wait_recv()

        @pl.when(self.onward(way))
        def _():
            self.hop(way, dist + 1, k).start()

    def sent(self, way):
        for dist in range(1, CHAIN):
            @pl.when(jnp.logical_and(self.onward(way), self.exists(way, dist - 1)))
            def _():
                for k in range(self.count):
                    self.hop(way, dist, k, own=dist == 1).wait_send()


def whole_kernel(
    pairs_ref, chol_ref, slabs_ref, r_ref, tr_ref,
    slot, cp, tc, ct, cts, yb, acc, ss1, rr1, ss2, rr2,
    local, outs, cz_s, cz_r, tz_s, tz_r, ag_s, ag_r, ct_s, ct_r, y_s, y_r, rs1_s, rs1_r, rs2_s, rs2_r,
):
    occ = r_ref.shape[0]
    _, size, wide = slabs_ref.shape
    depth = tall = occ * size
    half = wide // 2
    me, z = lax.axis_index("row"), lax.axis_index("col")
    core, chip = lax.rem(me, 2), me // 2
    xbit, ybit = lax.rem(chip, 2), chip // 2
    sib, xn, yn = me + 1 - 2 * core, me + 2 - 4 * xbit, me + 4 - 8 * ybit
    inner = jnp.logical_and(z > 0, z < CHAIN - 1)
    centre = 1 - (2 * z) // CHAIN

    def along(first):
        return xn + first * (yn - xn)

    barrier = pltpu.get_barrier_semaphore()

    def greet(where):
        pl.semaphore_signal(barrier, inc=1, device_id=where, device_id_type=MESH)

    for row in (sib, xn, yn):
        greet({"row": row})

    @pl.when(z > 0)
    def _():
        greet({"col": z - 1})

    @pl.when(z < CHAIN - 1)
    def _():
        greet({"col": z + 1})

    @pl.when(inner)
    def _():
        pl.semaphore_wait(barrier, 5)

    @pl.when(jnp.logical_not(inner))
    def _():
        pl.semaphore_wait(barrier, 4)

    chols = Chain(cp, chol_ref, occ, cz_s, cz_r)
    amps = Chain(tr_ref, slabs_ref, occ, tz_s, tz_r)
    cols = Gather(
        lambda low, count: tc.at[:, pl.ds(low, count), :],
        lambda low, count: slabs_ref.at[:, pl.ds(low, count), :],
        size, ag_s.at[occ], ag_r.at[occ],
    )
    chols.begin(0)
    chols.begin(1)
    cols.begin()
    keep_c = pltpu.make_async_copy(chol_ref, cp.at[z], local.at[0])
    keep_t = pltpu.make_async_copy(
        slabs_ref, tc.at[:, pl.ds(pl.multiple_of(me * size, size), size), :], local.at[1]
    )
    keep_c.start()
    keep_t.start()
    for pair in range(occ * occ):
        found = jnp.int32(0)
        for s in range(occ * occ):
            same = pairs_ref[s, 0] * occ + pairs_ref[s, 1] == pair
            found += s * same.astype(jnp.int32)
        slot[pair] = jnp.minimum(found, occ * occ - 1)
    keep_c.wait()
    keep_t.wait()

    def near(k, carry):
        for way in (0, 1):
            @pl.when(chols.exists(way, 1))
            def _():
                chols.arrive(way, 1, k)
        return carry

    lax.fori_loop(0, occ, near, 0)
    cols.relay()

    def piece_of(o, k):
        return cp[o, pl.ds(k * occ, occ)].reshape(depth, wide)

    def first_y(j, carry):
        acc[j] = piece_of(z, j).astype(F32)
        return carry

    lax.fori_loop(0, occ, first_y, 0)
    cols.last()
    cols.near()
    cols.distant()
    cols.sent()

    @pl.when(jnp.logical_not(inner))
    def _():
        chols.sent(centre)
        amps.begin(centre)

    def turned(o, k):
        return remote(
            cts.at[k], ct.at[o, core, pl.ds(pl.multiple_of(k * size, size), size), :],
            ct_s.at[k], ct_r.at[o, k], {"row": sib},
        )

    def turn(o, k):
        def half_of(which):
            block = cp[o, pl.ds(k * occ, occ), :, pl.ds(pl.multiple_of(which * size, size), size)]
            return jnp.transpose(block.reshape(depth, size), (1, 0))

        cts[k] = half_of(1 - core)
        turned(o, k).start()
        ct[o, core, pl.ds(pl.multiple_of(k * size, size), size), :] = half_of(core)

    def add_y(o, k):
        def one(j, carry):
            acc[j] += times(piece_of(o, k), tc[slot[k * occ + j], pl.ds(pl.multiple_of(o * wide, wide), wide), :])
            return carry

        lax.fori_loop(0, occ, one, 0)

    far_dist = jnp.where(inner, CHAIN // 2, CHAIN - 1)
    far_tile = chols.origin(1 - centre, far_dist)

    def come(event, waiting):
        dist, way = (event + 1) // 2, lax.rem(event + 1, 2)
        origin = chols.origin(way, dist)

        @pl.when(chols.exists(way, dist))
        def _():
            def step(k, carry):
                if waiting:
                    chols.arrive(way, dist, k)

                add_y(origin, k)

                @pl.when(event > 0)
                def _():
                    turned(origin, k).wait_send()

                if waiting:
                    @pl.when(jnp.logical_or(origin != far_tile, k < occ - 1))
                    def _():
                        turn(origin, k)
                else:
                    turn(origin, k)
                return carry

            lax.fori_loop(0, occ, step, 0)

    def here(event, carry):
        come(event, False)
        return carry

    def later(event, carry):
        come(event, True)
        return carry

    lax.fori_loop(0, 3, here, 0)
    lax.fori_loop(3, 2 * CHAIN - 1, later, 0)

    def y_copy(j):
        mine = yb.at[j, pl.ds(pl.multiple_of(core * depth, depth), depth), :]
        return remote(mine, mine, y_s.at[j], y_r.at[j], {"row": sib})

    def round_y(j, carry):
        yb[j, pl.ds(pl.multiple_of(core * depth, depth), depth), :] = acc[j].astype(BF16)
        y_copy(j).start()
        return carry

    lax.fori_loop(0, occ, round_y, 0)
    turn(far_tile, occ - 1)

    @pl.when(inner)
    def _():
        chols.sent(centre)
        amps.begin(centre)

    def turned_done(k, carry):
        turned(z, k).wait_send()
        for o in range(CHAIN):
            turned(o, k).wait_recv()
        return carry

    lax.fori_loop(0, occ, turned_done, 0)

    def side(first):
        return pl.ds(pl.multiple_of(first * half, half), half)

    def partial(q, j, first):
        return times(ct[q, 0], yb[j, :depth, side(first)]) + times(ct[q, 1], yb[j, depth:, side(first)])

    def rs1(first, j):
        return remote(
            ss1.at[first, j % 2], rr1.at[first, j], rs1_s.at[first, j], rs1_r.at[first, j],
            {"row": along(first)},
        )

    def rs2(first, j):
        return remote(
            ss2.at[first, j % 2], rr2.at[first, j], rs2_s.at[first, j], rs2_r.at[first, j],
            {"row": along(1 - first)},
        )

    def scatter_one(j):
        y_copy(j).wait_recv()
        for first in (0, 1):
            if j > 1:
                rs1(first, j - 2).wait_send()

            def each(n, carry):
                q = (2 * n + 1 - xbit) if first == 0 else (2 * (1 - ybit) + n)
                ss1[first, j % 2, n] = partial(q, j, first).astype(BF16)
                return carry

            lax.fori_loop(0, 2, each, 0)
            rs1(first, j).start()

    def scatter_two(j):
        if j > 1:
            for first in (0, 1):
                rs2(first, j - 2).wait_send()

        def each(first, carry):
            rs1(first, j).wait_recv()
            other = (1 - ybit) + first * (ybit - xbit)
            block = partial(along(1 - first) // 2, j, first) + rr1[first, j, other].astype(F32)
            ss2[first, j % 2] = block.astype(BF16)
            rs2(first, j).start()
            return carry

        lax.fori_loop(0, 2, each, 0)

    def scatter_end(j):
        def each(first, carry):
            mine = ybit + first * (xbit - ybit)
            block = partial(chip, j, first) + rr1[first, j, mine].astype(F32)
            rs2(first, j).wait_recv()
            block += rr2[first, j].astype(F32)
            acc[j, :, side(first)] = block
            for k in range(occ):
                tc[j * occ + k, pl.ds(pl.multiple_of(me * size, size), size), side(first)] = (
                    block[k * size:(k + 1) * size].astype(BF16)
                )
            return carry

        lax.fori_loop(0, 2, each, 0)

    def gather_of(j):
        def view(low, count):
            return tc.at[j * occ:(j + 1) * occ, pl.ds(low, count), :]

        return Gather(view, lambda low, count: view(pl.multiple_of(me * size + low, 16), count), size, ag_s.at[j], ag_r.at[j])

    gathers = [gather_of(j) for j in range(occ)]

    def bring(dist, own=False):
        if own:
            copy = pltpu.make_async_copy(slabs_ref, cp.at[z], local.at[0])
            copy.start()
            copy.wait()
            return
        for way in (0, 1):
            @pl.when(amps.exists(way, dist))
            def _():
                def step(k, carry):
                    amps.arrive(way, dist, k)
                    return carry

                lax.fori_loop(0, occ, step, 0)
                origin = amps.origin(way, dist)
                copy = pltpu.make_async_copy(tr_ref.at[origin], cp.at[origin], local.at[0])
                copy.start()
                copy.wait()

    def add_r(origin, j):
        def step(k, carry):
            left = jnp.concatenate([cp[origin, slot[i * occ + k]] for i in range(occ)], axis=0)
            acc[j] += times(left, tc[j * occ + k, pl.ds(pl.multiple_of(origin * wide, wide), wide), :])
            return carry

        lax.fori_loop(0, occ, step, 0)

    def product(low, high, first, last):
        def each(event, carry):
            dist, way = (event + 1) // 2, lax.rem(event + 1, 2)
            origin = chols.origin(way, dist)

            @pl.when(chols.exists(way, dist))
            def _():
                def step(n, inside):
                    add_r(origin, first + n)
                    return inside

                lax.fori_loop(0, last - first, step, 0)

            return carry

        lax.fori_loop(low, high, each, 0)

    def product_of(low, high, j):
        def each(n, carry):
            x = xbit + lax.rem(n, 2) * (1 - 2 * xbit)
            y = ybit + (n // 2) * (1 - 2 * ybit)
            add_r(2 * y + x, j)
            return carry

        lax.fori_loop(low, high, each, 0)

    def hand_out(j):
        return pltpu.make_async_copy(acc.at[j], r_ref.at[j], outs.at[j])

    scatter_one(0)
    scatter_one(1)
    scatter_two(0)
    scatter_one(2)
    scatter_two(1)
    scatter_end(0)
    gathers[0].begin()
    chols.sent(1 - centre)

    @pl.when(inner)
    def _():
        amps.begin(1 - centre)

    scatter_two(2)
    scatter_end(1)
    gathers[1].begin()
    bring(0, own=True)
    gathers[0].relay()
    scatter_end(2)
    gathers[2].begin()
    bring(1)
    gathers[1].relay()
    gathers[0].last()
    gathers[0].near()
    gathers[0].distant()
    product(0, 3, 0, 1)
    bring(2)
    gathers[2].relay()
    gathers[1].last()
    gathers[1].near()
    gathers[1].distant()
    product(0, 3, 1, 2)
    product(3, 5, 0, 2)
    bring(3)
    product(5, 7, 0, 2)
    hand_out(0).start()
    hand_out(1).start()
    gathers[2].last()
    gathers[2].near()
    product_of(0, 3, 2)
    gathers[2].distant()
    product_of(3, 4, 2)
    hand_out(2).start()
    for j in range(occ):
        gathers[j].sent()
    for first in (0, 1):
        for j in (1, 2):
            rs1(first, j).wait_send()
            rs2(first, j).wait_send()

    def y_done(j, carry):
        y_copy(j).wait_send()
        return carry

    lax.fori_loop(0, occ, y_done, 0)
    amps.sent(0)
    amps.sent(1)
    for j in range(occ):
        hand_out(j).wait()


def in_one_kernel(chol, amps, pairs):
    occ, depth, wide = chol.shape
    _, size, _ = amps.shape
    tall, full = occ * size, size * PLANE
    half = wide // 2
    dma = pltpu.SemaphoreType.DMA
    result, _ = pl.pallas_call(
        whole_kernel,
        out_shape=(
            jax.ShapeDtypeStruct((occ, tall, wide), F32),
            jax.ShapeDtypeStruct((CHAIN, occ * occ, size, wide), BF16),
        ),
        in_specs=[pl.BlockSpec(memory_space=pltpu.SMEM)] + [pl.BlockSpec(memory_space=pl.ANY)] * 2,
        out_specs=(pl.BlockSpec(memory_space=pl.ANY), pl.BlockSpec(memory_space=pl.ANY)),
        scratch_shapes=[
            pltpu.SMEM((occ * occ,), jnp.int32),
            pltpu.VMEM((CHAIN, occ * occ, size, wide), BF16),
            pltpu.VMEM((occ * occ, full, wide), BF16),
            pltpu.VMEM((CHAIN, 2, tall, depth), BF16),
            pltpu.VMEM((occ, size, depth), BF16),
            pltpu.VMEM((occ, 2 * depth, wide), BF16),
            pltpu.VMEM((occ, tall, wide), F32),
            pltpu.VMEM((2, 2, 2, tall, half), BF16),
            pltpu.VMEM((2, occ, 2, tall, half), BF16),
            pltpu.VMEM((2, 2, tall, half), BF16),
            pltpu.VMEM((2, occ, tall, half), BF16),
            dma((2,)),
            dma((occ,)),
            dma((2, CHAIN - 1, occ)),
            dma((2, CHAIN - 1, occ)),
            dma((2, CHAIN - 1, occ)),
            dma((2, CHAIN - 1, occ)),
            dma((occ + 1, PIECES)),
            dma((occ + 1, PIECES)),
            dma((occ,)),
            dma((CHAIN, occ)),
            dma((occ,)),
            dma((occ,)),
            dma((2, occ)),
            dma((2, occ)),
            dma((2, occ)),
            dma((2, occ)),
        ],
        compiler_params=pltpu.CompilerParams(
            collective_id=0, has_side_effects=True, vmem_limit_bytes=62 * 1024 * 1024
        ),
        cost_estimate=pl.CostEstimate(
            flops=6 * occ * depth * occ * full * wide, bytes_accessed=32 * chol.size, transcendentals=0
        ),
        name="whole",
    )(pairs, chol.reshape(amps.shape), amps)
    return result.reshape(occ * occ, size, wide)


def in_steps(chol, amps, pairs):
    occ, depth, _ = chol.shape
    _, size, wide = amps.shape
    order = jnp.arange(occ * occ, dtype=jnp.int32)
    flat_pair = pairs[:, 0] * occ + pairs[:, 1]
    matches = (flat_pair[None, :] == order[:, None]).astype(jnp.int32)
    grid = jnp.take(amps, jnp.sum(matches * order[None, :], axis=1), axis=0, mode="clip")
    slabs = grid.reshape(occ, occ, size, wide)
    cols = lax.all_gather(slabs, "row", axis=2, tiled=True)
    chol_rows = lax.all_gather(chol, "col", axis=2, tiled=True)
    y = lax.dot_general(chol_rows, cols, (((0, 2), (0, 2)), ((), ())), preferred_element_type=F32)
    y = (y + jnp.transpose(chol, (1, 0, 2)).astype(F32)).astype(BF16)
    swapped = lax.all_to_all(chol_rows, "row", split_axis=2, concat_axis=1, tiled=True)
    y = lax.all_gather(y.reshape(depth, occ * wide), "row", axis=0, tiled=True)
    dressed = lax.dot_general(swapped, y, (((1,), (0,)), ((), ())), preferred_element_type=F32)
    dressed_cols = lax.all_gather(dressed.astype(BF16), "row", axis=1, tiled=True)
    rows = lax.all_gather(slabs, "col", axis=3, tiled=True)
    total = lax.dot_general(rows, dressed_cols, (((1, 3), (0, 1)), ((), ())), preferred_element_type=F32)
    total = (total + dressed).reshape(occ, size, occ, wide)
    return jnp.transpose(total, (2, 0, 1, 3)).reshape(occ * occ, size, wide)


def close_kernel(pairs_ref, levels_ref, vir_ref, r_ref, amp_ref, out_ref, base):
    s = pl.program_id(0)
    size, wide = base.shape

    @pl.when(s == 0)
    def _():
        rows = vir_ref[:, pl.ds(pl.multiple_of(lax.axis_index("row") * size, size), size)]
        cols = vir_ref[:, pl.ds(pl.multiple_of(lax.axis_index("col") * wide, wide), wide)]
        rows = jnp.transpose(jnp.broadcast_to(rows, (128, size)), (1, 0))
        base[...] = rows[:, :1] + cols

    levels = levels_ref[pairs_ref[s, 0]] + levels_ref[pairs_ref[s, 1]]
    out_ref[0] = r_ref[0] + (base[...] - levels) * amp_ref[0].astype(F32)


def close(product, amps, eps_occ, eps_vir, pairs):
    slabs, size, wide = amps.shape
    occ = eps_occ.shape[0]
    block = (1, size, wide)
    return pl.pallas_call(
        close_kernel,
        out_shape=jax.ShapeDtypeStruct(amps.shape, F32),
        grid_spec=pltpu.PrefetchScalarGridSpec(
            num_scalar_prefetch=1,
            grid=(slabs,),
            in_specs=[
                pl.BlockSpec(memory_space=pltpu.SMEM),
                pl.BlockSpec((1, eps_vir.shape[0]), lambda s, pairs: (0, 0)),
                pl.BlockSpec(block, lambda s, pairs: (pairs[s, 1] * occ + pairs[s, 0], 0, 0)),
                pl.BlockSpec(block, lambda s, pairs: (s, 0, 0)),
            ],
            out_specs=pl.BlockSpec(block, lambda s, pairs: (s, 0, 0)),
            scratch_shapes=[pltpu.VMEM((size, wide), F32)],
        ),
        name="close",
    )(pairs, eps_occ, eps_vir.reshape(1, -1), product, amps)


def per_device(chol, amps, eps_occ, eps_vir, pairs):
    occ, depth, wide = chol.shape
    size = amps.shape[1]
    one = lax.axis_size("row") == PLANE and lax.axis_size("col") == CHAIN
    one = one and depth == occ * size and wide == 2 * size
    product = (in_one_kernel if one else in_steps)(chol, amps, pairs)
    return close(product, amps, eps_occ, eps_vir, pairs)


def solution(mesh):
    placed = (P(None, "row", "col"), P(None, "row", "col"), P(), P(), P())
    return jax.shard_map(
        per_device, mesh=mesh, in_specs=placed, out_specs=P(None, "row", "col"), check_vma=False
    )
```

```python
import functools

import jax
import jax.numpy as jnp
from jax import lax
from jax.experimental import pallas as pl
from jax.experimental.pallas import tpu as pltpu
from jax.sharding import PartitionSpec as P

F32 = jnp.float32
BF16 = jnp.bfloat16
MESH = pl.DeviceIdType.MESH
PLANE = 8
CHAIN = 4
PIECES = 11


def remote(src, dst, send, recv, where):
    return pltpu.make_async_remote_copy(
        src_ref=src, dst_ref=dst, send_sem=send, recv_sem=recv, device_id=where, device_id_type=MESH
    )


def times(left, right):
    return jnp.dot(left, right, preferred_element_type=F32)


class Gather:
    def __init__(self, view, own, size, send, recv):
        me = lax.axis_index("row")
        core, xbit, ybit = lax.rem(me, 2), lax.rem(me // 2, 2), me // 4
        sib, xn, yn = me + 1 - 2 * core, me + 2 - 4 * xbit, me + 4 - 8 * ybit
        far = xn + 4 - 8 * ybit
        half = size // 2

        def part(origin, low, count):
            return view(pl.multiple_of(origin * size + low, 16), count)

        def make(index, src, dst, where):
            return remote(src, dst, send.at[index], recv.at[index], {"row": where})

        def hand_on(index, origin, low, count, where):
            return make(index, part(origin, low, count), part(origin, low, count), where)

        self.copies = [
            make(0, own(0, half), part(me, 0, half), xn),
            make(1, own(half, half), part(me, half, half), xn),
            make(2, own(half, half), part(me, half, half), yn),
            make(3, own(0, half), part(me, 0, half), yn),
            make(4, own(0, size), part(me, 0, size), sib),
            hand_on(5, xn, 0, half, yn),
            hand_on(6, yn, half, half, xn),
            hand_on(7, xn, 0, size, sib),
            hand_on(8, yn, 0, size, sib),
            hand_on(9, far, 0, half, sib),
            hand_on(10, far, half, half, sib),
        ]

    def begin(self):
        for index in (0, 2, 1, 3, 4):
            self.copies[index].start()

    def relay(self):
        for arrived, onward in ((0, 5), (2, 6), (1, 7), (3, 8)):
            self.copies[arrived].wait_recv()
            self.copies[onward].start()

    def last(self):
        for arrived, onward in ((5, 9), (6, 10)):
            self.copies[arrived].wait_recv()
            self.copies[onward].start()

    def near(self):
        for index in (4, 7, 8):
            self.copies[index].wait_recv()

    def distant(self):
        for index in (9, 10):
            self.copies[index].wait_recv()

    def sent(self):
        for copy in self.copies:
            copy.wait_send()


class Chain:
    def __init__(self, panel, own, count, send, recv):
        self.panel, self.own, self.count, self.send, self.recv = panel, own, count, send, recv
        self.z = lax.axis_index("col")

    def piece(self, k):
        return pl.ds(k * self.count, self.count)

    def origin(self, way, dist):
        return self.z + dist * (1 - 2 * way)

    def exists(self, way, dist):
        origin = self.origin(way, dist)
        return jnp.logical_and(origin >= 0, origin < CHAIN)

    def onward(self, way):
        return self.exists(1 - way, 1)

    def hop(self, way, dist, k, own=False):
        origin = self.z if own else self.origin(way, dist - 1)
        src = self.own.at[self.piece(k)] if own else self.panel.at[origin, self.piece(k)]
        where = {"col": self.z - 1 + 2 * way}
        return remote(
            src, self.panel.at[origin, self.piece(k)], self.send.at[way, dist - 1, k], self.recv.at[way, dist - 1, k], where
        )

    def begin(self, way):
        @pl.when(self.onward(way))
        def _():
            for k in range(self.count):
                self.hop(way, 1, k, own=True).start()

    def arrive(self, way, dist, k):
        origin = self.origin(way, dist)
        sem = (way, dist - 1, k)
        remote(
            self.panel.at[origin, self.piece(k)], self.panel.at[origin, self.piece(k)],
            self.send.at[sem], self.recv.at[sem], {"col": origin},
        ).wait_recv()

        @pl.when(self.onward(way))
        def _():
            self.hop(way, dist + 1, k).start()

    def sent(self, way):
        for dist in range(1, CHAIN):
            @pl.when(jnp.logical_and(self.onward(way), self.exists(way, dist - 1)))
            def _():
                for k in range(self.count):
                    self.hop(way, dist, k, own=dist == 1).wait_send()


def whole_kernel(
    pairs_ref, chol_ref, slabs_ref, r_ref, tr_ref,
    slot, cp, tc, ct, cts, yb, acc, ss1, rr1, ss2, rr2,
    local, outs, cz_s, cz_r, tz_s, tz_r, ag_s, ag_r, ct_s, ct_r, y_s, y_r, rs1_s, rs1_r, rs2_s, rs2_r,
):
    occ = r_ref.shape[0]
    _, size, wide = slabs_ref.shape
    depth = tall = occ * size
    half = wide // 2
    me, z = lax.axis_index("row"), lax.axis_index("col")
    core, chip = lax.rem(me, 2), me // 2
    xbit, ybit = lax.rem(chip, 2), chip // 2
    sib, xn, yn = me + 1 - 2 * core, me + 2 - 4 * xbit, me + 4 - 8 * ybit
    inner = jnp.logical_and(z > 0, z < CHAIN - 1)
    centre = 1 - (2 * z) // CHAIN

    def along(first):
        return xn + first * (yn - xn)

    barrier = pltpu.get_barrier_semaphore()

    def greet(where):
        pl.semaphore_signal(barrier, inc=1, device_id=where, device_id_type=MESH)

    for row in (sib, xn, yn):
        greet({"row": row})

    @pl.when(z > 0)
    def _():
        greet({"col": z - 1})

    @pl.when(z < CHAIN - 1)
    def _():
        greet({"col": z + 1})

    @pl.when(inner)
    def _():
        pl.semaphore_wait(barrier, 5)

    @pl.when(jnp.logical_not(inner))
    def _():
        pl.semaphore_wait(barrier, 4)

    chols = Chain(cp, chol_ref, occ, cz_s, cz_r)
    amps = Chain(tr_ref, slabs_ref, occ, tz_s, tz_r)
    cols = Gather(
        lambda low, count: tc.at[:, pl.ds(low, count), :],
        lambda low, count: slabs_ref.at[:, pl.ds(low, count), :],
        size, ag_s.at[occ], ag_r.at[occ],
    )
    chols.begin(0)
    chols.begin(1)
    cols.begin()
    keep_c = pltpu.make_async_copy(chol_ref, cp.at[z], local.at[0])
    keep_t = pltpu.make_async_copy(
        slabs_ref, tc.at[:, pl.ds(pl.multiple_of(me * size, size), size), :], local.at[1]
    )
    keep_c.start()
    keep_t.start()
    for pair in range(occ * occ):
        found = jnp.int32(0)
        for s in range(occ * occ):
            same = pairs_ref[0, s] * occ + pairs_ref[1, s] == pair
            found += s * same.astype(jnp.int32)
        slot[pair] = jnp.minimum(found, occ * occ - 1)
    keep_c.wait()
    keep_t.wait()

    def near(k, carry):
        for way in (0, 1):
            @pl.when(chols.exists(way, 1))
            def _():
                chols.arrive(way, 1, k)
        return carry

    lax.fori_loop(0, occ, near, 0)
    cols.relay()

    def piece_of(o, k):
        return cp[o, pl.ds(k * occ, occ)].reshape(depth, wide)

    def first_y(j, carry):
        acc[j] = piece_of(z, j).astype(F32)
        return carry

    lax.fori_loop(0, occ, first_y, 0)
    cols.last()
    cols.near()
    cols.distant()
    cols.sent()

    @pl.when(jnp.logical_not(inner))
    def _():
        chols.sent(centre)
        amps.begin(centre)

    mine = pl.ds(pl.multiple_of(core * depth, depth), depth)

    def turned(o, k):
        return remote(
            cts.at[k], ct.at[o, pl.ds(pl.multiple_of(k * size, size), size), mine],
            ct_s.at[k], ct_r.at[o, k], {"row": sib},
        )

    def turn(o, k):
        def half_of(which):
            block = cp[o, pl.ds(k * occ, occ), :, pl.ds(pl.multiple_of(which * size, size), size)]
            return jnp.transpose(block.reshape(depth, size), (1, 0))

        cts[k] = half_of(1 - core)
        turned(o, k).start()
        ct[o, pl.ds(pl.multiple_of(k * size, size), size), mine] = half_of(core)

    def add_y(o, k):
        def one(j, carry):
            acc[j] += times(piece_of(o, k), tc[slot[k * occ + j], pl.ds(pl.multiple_of(o * wide, wide), wide), :])
            return carry

        lax.fori_loop(0, occ, one, 0)

    far_dist = jnp.where(inner, CHAIN // 2, CHAIN - 1)
    far_tile = chols.origin(1 - centre, far_dist)

    def come(event, waiting):
        dist, way = (event + 1) // 2, lax.rem(event + 1, 2)
        origin = chols.origin(way, dist)

        @pl.when(chols.exists(way, dist))
        def _():
            def step(k, carry):
                if waiting:
                    chols.arrive(way, dist, k)

                add_y(origin, k)

                @pl.when(event > 0)
                def _():
                    turned(origin, k).wait_send()

                if waiting:
                    @pl.when(jnp.logical_or(origin != far_tile, k < occ - 1))
                    def _():
                        turn(origin, k)
                else:
                    turn(origin, k)
                return carry

            lax.fori_loop(0, occ, step, 0)

    def here(event, carry):
        come(event, False)
        return carry

    def later(event, carry):
        come(event, True)
        return carry

    lax.fori_loop(0, 3, here, 0)
    lax.fori_loop(3, 2 * CHAIN - 1, later, 0)

    def y_copy(j):
        own = yb.at[j, mine, :]
        return remote(own, own, y_s.at[j], y_r.at[j], {"row": sib})

    def round_y(j, carry):
        yb[j, mine, :] = acc[j].astype(BF16)
        y_copy(j).start()
        return carry

    lax.fori_loop(0, occ, round_y, 0)
    turn(far_tile, occ - 1)

    @pl.when(inner)
    def _():
        chols.sent(centre)
        amps.begin(centre)

    def turned_done(k, carry):
        turned(z, k).wait_send()
        for o in range(CHAIN):
            turned(o, k).wait_recv()
        return carry

    lax.fori_loop(0, occ, turned_done, 0)

    def side(first):
        return pl.ds(pl.multiple_of(first * half, half), half)

    def partial(q, j, first):
        return times(ct[q], yb[j, :, side(first)])

    def rs1(first, j):
        return remote(
            ss1.at[first, j % 2], rr1.at[first, j], rs1_s.at[first, j], rs1_r.at[first, j],
            {"row": along(first)},
        )

    def rs2(first, j):
        return remote(
            ss2.at[first, j % 2], rr2.at[first, j], rs2_s.at[first, j], rs2_r.at[first, j],
            {"row": along(1 - first)},
        )

    def scatter_one(j):
        y_copy(j).wait_recv()
        for first in (0, 1):
            if j > 1:
                rs1(first, j - 2).wait_send()

            def each(n, carry):
                q = (2 * n + 1 - xbit) if first == 0 else (2 * (1 - ybit) + n)
                ss1[first, j % 2, n] = partial(q, j, first).astype(BF16)
                return carry

            lax.fori_loop(0, 2, each, 0)
            rs1(first, j).start()

    def scatter_two(j):
        if j > 1:
            for first in (0, 1):
                rs2(first, j - 2).wait_send()

        def each(first, carry):
            rs1(first, j).wait_recv()
            other = (1 - ybit) + first * (ybit - xbit)
            block = partial(along(1 - first) // 2, j, first) + rr1[first, j, other].astype(F32)
            ss2[first, j % 2] = block.astype(BF16)
            rs2(first, j).start()
            return carry

        lax.fori_loop(0, 2, each, 0)

    def scatter_end(j):
        def each(first, carry):
            own = ybit + first * (xbit - ybit)
            block = partial(chip, j, first) + rr1[first, j, own].astype(F32)
            rs2(first, j).wait_recv()
            block += rr2[first, j].astype(F32)
            acc[j, :, side(first)] = block
            for k in range(occ):
                tc[j * occ + k, pl.ds(pl.multiple_of(me * size, size), size), side(first)] = (
                    block[k * size:(k + 1) * size].astype(BF16)
                )
            return carry

        lax.fori_loop(0, 2, each, 0)

    def gather_of(j):
        def view(low, count):
            return tc.at[j * occ:(j + 1) * occ, pl.ds(low, count), :]

        return Gather(view, lambda low, count: view(pl.multiple_of(me * size + low, 16), count), size, ag_s.at[j], ag_r.at[j])

    gathers = [gather_of(j) for j in range(occ)]

    def bring(dist, own=False):
        if own:
            copy = pltpu.make_async_copy(slabs_ref, cp.at[z], local.at[0])
            copy.start()
            copy.wait()
            return
        for way in (0, 1):
            @pl.when(amps.exists(way, dist))
            def _():
                def step(k, carry):
                    amps.arrive(way, dist, k)
                    return carry

                lax.fori_loop(0, occ, step, 0)
                origin = amps.origin(way, dist)
                copy = pltpu.make_async_copy(tr_ref.at[origin], cp.at[origin], local.at[0])
                copy.start()
                copy.wait()

    def add_r(origin, j):
        right = tc[pl.ds(j * occ, occ), pl.ds(pl.multiple_of(origin * wide, wide), wide), :].reshape(occ * wide, wide)
        for i in range(occ):
            left = jnp.concatenate([cp[origin, slot[i * occ + k]] for k in range(occ)], axis=1)
            acc[j, i * size:(i + 1) * size] += times(left, right)

    def product(low, high, first, last):
        def each(event, carry):
            dist, way = (event + 1) // 2, lax.rem(event + 1, 2)
            origin = chols.origin(way, dist)

            @pl.when(chols.exists(way, dist))
            def _():
                def step(n, inside):
                    add_r(origin, first + n)
                    return inside

                lax.fori_loop(0, last - first, step, 0)

            return carry

        lax.fori_loop(low, high, each, 0)

    def product_of(low, high, j):
        def each(n, carry):
            x = xbit + lax.rem(n, 2) * (1 - 2 * xbit)
            y = ybit + (n // 2) * (1 - 2 * ybit)
            add_r(2 * y + x, j)
            return carry

        lax.fori_loop(low, high, each, 0)

    def hand_out(j):
        return pltpu.make_async_copy(acc.at[j], r_ref.at[j], outs.at[j])

    scatter_one(0)
    scatter_one(1)
    scatter_two(0)
    scatter_one(2)
    scatter_two(1)
    scatter_end(0)
    gathers[0].begin()
    chols.sent(1 - centre)

    @pl.when(inner)
    def _():
        amps.begin(1 - centre)

    scatter_two(2)
    scatter_end(1)
    gathers[1].begin()
    bring(0, own=True)
    gathers[0].relay()
    scatter_end(2)
    gathers[2].begin()
    bring(1)
    gathers[1].relay()
    gathers[0].last()
    gathers[0].near()
    gathers[0].distant()
    product(0, 3, 0, 1)
    bring(2)
    product(3, 5, 0, 1)
    gathers[1].last()
    gathers[1].near()
    gathers[1].distant()
    gathers[2].relay()
    product(0, 5, 1, 2)
    bring(3)
    product(5, 7, 0, 2)
    hand_out(0).start()
    hand_out(1).start()
    gathers[2].last()
    gathers[2].near()
    product_of(0, 3, 2)
    gathers[2].distant()
    product_of(3, 4, 2)
    hand_out(2).start()
    for j in range(occ):
        gathers[j].sent()
    for first in (0, 1):
        for j in (1, 2):
            rs1(first, j).wait_send()
            rs2(first, j).wait_send()

    def y_done(j, carry):
        y_copy(j).wait_send()
        return carry

    lax.fori_loop(0, occ, y_done, 0)
    amps.sent(0)
    amps.sent(1)
    for j in range(occ):
        hand_out(j).wait()


def in_one_kernel(chol, amps, pairs):
    occ, depth, wide = chol.shape
    _, size, _ = amps.shape
    tall, full = occ * size, size * PLANE
    half = wide // 2
    dma = pltpu.SemaphoreType.DMA
    result, _ = pl.pallas_call(
        whole_kernel,
        out_shape=(
            jax.ShapeDtypeStruct((occ, tall, wide), F32),
            jax.ShapeDtypeStruct((CHAIN, occ * occ, size, wide), BF16),
        ),
        in_specs=[pl.BlockSpec(memory_space=pltpu.SMEM)] + [pl.BlockSpec(memory_space=pl.ANY)] * 2,
        out_specs=(pl.BlockSpec(memory_space=pl.ANY), pl.BlockSpec(memory_space=pl.ANY)),
        scratch_shapes=[
            pltpu.SMEM((occ * occ,), jnp.int32),
            pltpu.VMEM((CHAIN, occ * occ, size, wide), BF16),
            pltpu.VMEM((occ * occ, full, wide), BF16),
            pltpu.VMEM((CHAIN, tall, 2 * depth), BF16),
            pltpu.VMEM((occ, size, depth), BF16),
            pltpu.VMEM((occ, 2 * depth, wide), BF16),
            pltpu.VMEM((occ, tall, wide), F32),
            pltpu.VMEM((2, 2, 2, tall, half), BF16),
            pltpu.VMEM((2, occ, 2, tall, half), BF16),
            pltpu.VMEM((2, 2, tall, half), BF16),
            pltpu.VMEM((2, occ, tall, half), BF16),
            dma((2,)),
            dma((occ,)),
            dma((2, CHAIN - 1, occ)),
            dma((2, CHAIN - 1, occ)),
            dma((2, CHAIN - 1, occ)),
            dma((2, CHAIN - 1, occ)),
            dma((occ + 1, PIECES)),
            dma((occ + 1, PIECES)),
            dma((occ,)),
            dma((CHAIN, occ)),
            dma((occ,)),
            dma((occ,)),
            dma((2, occ)),
            dma((2, occ)),
            dma((2, occ)),
            dma((2, occ)),
        ],
        compiler_params=pltpu.CompilerParams(
            collective_id=0, has_side_effects=True, vmem_limit_bytes=62 * 1024 * 1024
        ),
        cost_estimate=pl.CostEstimate(
            flops=6 * occ * depth * occ * full * wide, bytes_accessed=32 * chol.size, transcendentals=0
        ),
        name="whole",
    )(pairs.T, chol.reshape(amps.shape), amps)
    return result.reshape(occ * occ, size, wide)


def in_steps(chol, amps, pairs):
    occ, depth, _ = chol.shape
    _, size, wide = amps.shape
    order = jnp.arange(occ * occ, dtype=jnp.int32)
    flat_pair = pairs[:, 0] * occ + pairs[:, 1]
    matches = (flat_pair[None, :] == order[:, None]).astype(jnp.int32)
    grid = jnp.take(amps, jnp.sum(matches * order[None, :], axis=1), axis=0, mode="clip")
    slabs = grid.reshape(occ, occ, size, wide)
    cols = lax.all_gather(slabs, "row", axis=2, tiled=True)
    chol_rows = lax.all_gather(chol, "col", axis=2, tiled=True)
    y = lax.dot_general(chol_rows, cols, (((0, 2), (0, 2)), ((), ())), preferred_element_type=F32)
    y = (y + jnp.transpose(chol, (1, 0, 2)).astype(F32)).astype(BF16)
    swapped = lax.all_to_all(chol_rows, "row", split_axis=2, concat_axis=1, tiled=True)
    y = lax.all_gather(y.reshape(depth, occ * wide), "row", axis=0, tiled=True)
    dressed = lax.dot_general(swapped, y, (((1,), (0,)), ((), ())), preferred_element_type=F32)
    dressed_cols = lax.all_gather(dressed.astype(BF16), "row", axis=1, tiled=True)
    rows = lax.all_gather(slabs, "col", axis=3, tiled=True)
    total = lax.dot_general(rows, dressed_cols, (((1, 3), (0, 1)), ((), ())), preferred_element_type=F32)
    total = (total + dressed).reshape(occ, size, occ, wide)
    return jnp.transpose(total, (2, 0, 1, 3)).reshape(occ * occ, size, wide)


def close_kernel(pairs_ref, levels_ref, vir_ref, r_ref, amp_ref, out_ref, base, r, amp, out, r_sem, amp_sem, out_sem):
    size, wide = base.shape
    occ = levels_ref.shape[0]
    slabs = r.shape[0]

    def load(s):
        index = pairs_ref[1, s] * occ + pairs_ref[0, s]
        return (
            pltpu.make_async_copy(r_ref.at[index], r.at[s], r_sem.at[s]),
            pltpu.make_async_copy(amp_ref.at[s], amp.at[s], amp_sem.at[s]),
        )

    def store(s):
        return pltpu.make_async_copy(out.at[s], out_ref.at[s], out_sem.at[s])

    for s in range(slabs):
        for copy in load(s):
            copy.start()
    rows = vir_ref[:, pl.ds(pl.multiple_of(lax.axis_index("row") * size, size), size)]
    cols = vir_ref[:, pl.ds(pl.multiple_of(lax.axis_index("col") * wide, wide), wide)]
    rows = jnp.transpose(jnp.broadcast_to(rows, (128, size)), (1, 0))
    base[...] = rows[:, :1] + cols

    def one(s, carry):
        for copy in load(s):
            copy.wait()
        levels = levels_ref[pairs_ref[0, s]] + levels_ref[pairs_ref[1, s]]
        out[s] = r[s] + (base[...] - levels) * amp[s].astype(F32)
        store(s).start()
        return carry

    lax.fori_loop(0, slabs, one, 0)
    for s in range(slabs):
        store(s).wait()


def close(product, amps, eps_occ, eps_vir, pairs):
    slabs, size, wide = amps.shape
    return pl.pallas_call(
        close_kernel,
        out_shape=jax.ShapeDtypeStruct(amps.shape, F32),
        in_specs=[
            pl.BlockSpec(memory_space=pltpu.SMEM),
            pl.BlockSpec(memory_space=pltpu.SMEM),
            pl.BlockSpec(memory_space=pltpu.VMEM),
            pl.BlockSpec(memory_space=pl.ANY),
            pl.BlockSpec(memory_space=pl.ANY),
        ],
        out_specs=pl.BlockSpec(memory_space=pl.ANY),
        scratch_shapes=[
            pltpu.VMEM((size, wide), F32),
            pltpu.VMEM(amps.shape, F32),
            pltpu.VMEM(amps.shape, BF16),
            pltpu.VMEM(amps.shape, F32),
            pltpu.SemaphoreType.DMA((slabs,)),
            pltpu.SemaphoreType.DMA((slabs,)),
            pltpu.SemaphoreType.DMA((slabs,)),
        ],
        compiler_params=pltpu.CompilerParams(vmem_limit_bytes=62 * 1024 * 1024),
        name="close",
    )(pairs.T, eps_occ, eps_vir.reshape(1, -1), product, amps)


def per_device(chol, amps, eps_occ, eps_vir, pairs):
    occ, depth, wide = chol.shape
    size = amps.shape[1]
    one = lax.axis_size("row") == PLANE and lax.axis_size("col") == CHAIN
    one = one and depth == occ * size and wide == 2 * size
    product = (in_one_kernel if one else in_steps)(chol, amps, pairs)
    return close(product, amps, eps_occ, eps_vir, pairs)


def solution(mesh):
    placed = (P(None, "row", "col"), P(None, "row", "col"), P(), P(), P())
    return jax.shard_map(
        per_device, mesh=mesh, in_specs=placed, out_specs=P(None, "row", "col"), check_vma=False
    )
```

```python
import functools

import jax
import jax.numpy as jnp
from jax import lax
from jax.experimental import pallas as pl
from jax.experimental.pallas import tpu as pltpu
from jax.sharding import PartitionSpec as P

F32 = jnp.float32
BF16 = jnp.bfloat16
MESH = pl.DeviceIdType.MESH
PLANE = 8
CHAIN = 4
PIECES = 11
AHEAD = 4


def remote(src, dst, send, recv, where):
    return pltpu.make_async_remote_copy(
        src_ref=src, dst_ref=dst, send_sem=send, recv_sem=recv, device_id=where, device_id_type=MESH
    )


def times(left, right):
    return jnp.dot(left, right, preferred_element_type=F32)


class Gather:
    def __init__(self, view, own, size, send, recv):
        me = lax.axis_index("row")
        core, xbit, ybit = lax.rem(me, 2), lax.rem(me // 2, 2), me // 4
        sib, xn, yn = me + 1 - 2 * core, me + 2 - 4 * xbit, me + 4 - 8 * ybit
        far = xn + 4 - 8 * ybit
        half = size // 2

        def part(origin, low, count):
            return view(pl.multiple_of(origin * size + low, 16), count)

        def make(index, src, dst, where):
            return remote(src, dst, send.at[index], recv.at[index], {"row": where})

        def hand_on(index, origin, low, count, where):
            return make(index, part(origin, low, count), part(origin, low, count), where)

        self.copies = [
            make(0, own(0, half), part(me, 0, half), xn),
            make(1, own(half, half), part(me, half, half), xn),
            make(2, own(half, half), part(me, half, half), yn),
            make(3, own(0, half), part(me, 0, half), yn),
            make(4, own(0, size), part(me, 0, size), sib),
            hand_on(5, xn, 0, half, yn),
            hand_on(6, yn, half, half, xn),
            hand_on(7, xn, 0, size, sib),
            hand_on(8, yn, 0, size, sib),
            hand_on(9, far, 0, half, sib),
            hand_on(10, far, half, half, sib),
        ]

    def begin(self):
        for index in (0, 2, 1, 3, 4):
            self.copies[index].start()

    def relay(self):
        for arrived, onward in ((0, 5), (2, 6), (1, 7), (3, 8)):
            self.copies[arrived].wait_recv()
            self.copies[onward].start()

    def last(self):
        for arrived, onward in ((5, 9), (6, 10)):
            self.copies[arrived].wait_recv()
            self.copies[onward].start()

    def near(self):
        for index in (4, 7, 8):
            self.copies[index].wait_recv()

    def distant(self):
        for index in (9, 10):
            self.copies[index].wait_recv()

    def sent(self):
        for copy in self.copies:
            copy.wait_send()


class Chain:
    def __init__(self, panel, own, count, send, recv):
        self.panel, self.own, self.count, self.send, self.recv = panel, own, count, send, recv
        self.z = lax.axis_index("col")

    def piece(self, k):
        return pl.ds(k * self.count, self.count)

    def origin(self, way, dist):
        return self.z + dist * (1 - 2 * way)

    def exists(self, way, dist):
        origin = self.origin(way, dist)
        return jnp.logical_and(origin >= 0, origin < CHAIN)

    def onward(self, way):
        return self.exists(1 - way, 1)

    def hop(self, way, dist, k, own=False):
        origin = self.z if own else self.origin(way, dist - 1)
        src = self.own.at[self.piece(k)] if own else self.panel.at[origin, self.piece(k)]
        where = {"col": self.z - 1 + 2 * way}
        return remote(
            src, self.panel.at[origin, self.piece(k)], self.send.at[way, dist - 1, k], self.recv.at[way, dist - 1, k], where
        )

    def begin(self, way):
        @pl.when(self.onward(way))
        def _():
            for k in range(self.count):
                self.hop(way, 1, k, own=True).start()

    def arrive(self, way, dist, k):
        origin = self.origin(way, dist)
        sem = (way, dist - 1, k)
        remote(
            self.panel.at[origin, self.piece(k)], self.panel.at[origin, self.piece(k)],
            self.send.at[sem], self.recv.at[sem], {"col": origin},
        ).wait_recv()

        @pl.when(self.onward(way))
        def _():
            self.hop(way, dist + 1, k).start()

    def sent(self, way):
        for dist in range(1, CHAIN):
            @pl.when(jnp.logical_and(self.onward(way), self.exists(way, dist - 1)))
            def _():
                for k in range(self.count):
                    self.hop(way, dist, k, own=dist == 1).wait_send()


def whole_kernel(
    pairs_ref, chol_ref, slabs_ref, r_ref, tr_ref,
    slot, cp, tc, ct, cts, yb, acc, ss1, rr1, ss2, rr2,
    local, outs, cz_s, cz_r, tz_s, tz_r, ag_s, ag_r, ct_s, ct_r, y_s, y_r, rs1_s, rs1_r, rs2_s, rs2_r,
):
    occ = r_ref.shape[0]
    _, size, wide = slabs_ref.shape
    depth = tall = occ * size
    half = wide // 2
    me, z = lax.axis_index("row"), lax.axis_index("col")
    core, chip = lax.rem(me, 2), me // 2
    xbit, ybit = lax.rem(chip, 2), chip // 2
    sib, xn, yn = me + 1 - 2 * core, me + 2 - 4 * xbit, me + 4 - 8 * ybit
    inner = jnp.logical_and(z > 0, z < CHAIN - 1)
    centre = 1 - (2 * z) // CHAIN

    def along(first):
        return xn + first * (yn - xn)

    barrier = pltpu.get_barrier_semaphore()

    def greet(where):
        pl.semaphore_signal(barrier, inc=1, device_id=where, device_id_type=MESH)

    for row in (sib, xn, yn):
        greet({"row": row})

    @pl.when(z > 0)
    def _():
        greet({"col": z - 1})

    @pl.when(z < CHAIN - 1)
    def _():
        greet({"col": z + 1})

    @pl.when(inner)
    def _():
        pl.semaphore_wait(barrier, 5)

    @pl.when(jnp.logical_not(inner))
    def _():
        pl.semaphore_wait(barrier, 4)

    chols = Chain(cp, chol_ref, occ, cz_s, cz_r)
    amps = Chain(tr_ref, slabs_ref, occ, tz_s, tz_r)
    cols = Gather(
        lambda low, count: tc.at[:, pl.ds(low, count), :],
        lambda low, count: slabs_ref.at[:, pl.ds(low, count), :],
        size, ag_s.at[occ], ag_r.at[occ],
    )
    chols.begin(0)
    chols.begin(1)
    cols.begin()
    keep_c = pltpu.make_async_copy(chol_ref, cp.at[z], local.at[0])
    keep_t = pltpu.make_async_copy(
        slabs_ref, tc.at[:, pl.ds(pl.multiple_of(me * size, size), size), :], local.at[1]
    )
    keep_c.start()
    keep_t.start()
    for pair in range(occ * occ):
        found = jnp.int32(0)
        for s in range(occ * occ):
            same = pairs_ref[0, s] * occ + pairs_ref[1, s] == pair
            found += s * same.astype(jnp.int32)
        slot[pair] = jnp.minimum(found, occ * occ - 1)
    keep_c.wait()
    keep_t.wait()

    def near(k, carry):
        for way in (0, 1):
            @pl.when(chols.exists(way, 1))
            def _():
                chols.arrive(way, 1, k)
        return carry

    lax.fori_loop(0, occ, near, 0)
    cols.relay()

    def piece_of(o, k):
        return cp[o, pl.ds(k * occ, occ)].reshape(depth, wide)

    def first_y(j, carry):
        acc[j] = piece_of(z, j).astype(F32)
        return carry

    lax.fori_loop(0, occ, first_y, 0)
    cols.last()
    cols.near()
    cols.distant()
    cols.sent()

    @pl.when(jnp.logical_not(inner))
    def _():
        chols.sent(centre)
        amps.begin(centre)

    mine = pl.ds(pl.multiple_of(core * depth, depth), depth)

    def turned(o, k):
        return remote(
            cts.at[k], ct.at[o, pl.ds(pl.multiple_of(k * size, size), size), mine],
            ct_s.at[k], ct_r.at[o, k], {"row": sib},
        )

    def turn(o, k):
        def half_of(which):
            block = cp[o, pl.ds(k * occ, occ), :, pl.ds(pl.multiple_of(which * size, size), size)]
            return jnp.transpose(block.reshape(depth, size), (1, 0))

        cts[k] = half_of(1 - core)
        turned(o, k).start()
        ct[o, pl.ds(pl.multiple_of(k * size, size), size), mine] = half_of(core)

    def add_y(o, k):
        def one(j, carry):
            acc[j] += times(piece_of(o, k), tc[slot[k * occ + j], pl.ds(pl.multiple_of(o * wide, wide), wide), :])
            return carry

        lax.fori_loop(0, occ, one, 0)

    far_dist = jnp.where(inner, CHAIN // 2, CHAIN - 1)
    far_tile = chols.origin(1 - centre, far_dist)

    def come(event, waiting):
        dist, way = (event + 1) // 2, lax.rem(event + 1, 2)
        origin = chols.origin(way, dist)

        @pl.when(chols.exists(way, dist))
        def _():
            def step(k, carry):
                if waiting:
                    chols.arrive(way, dist, k)

                @pl.when(event > 0)
                def _():
                    turned(origin, k).wait_send()

                if waiting:
                    @pl.when(jnp.logical_or(origin != far_tile, k < occ - 1))
                    def _():
                        turn(origin, k)
                        add_y(origin, k)
                else:
                    turn(origin, k)
                    add_y(origin, k)
                return carry

            lax.fori_loop(0, occ, step, 0)

    def here(event, carry):
        come(event, False)
        return carry

    def later(event, carry):
        come(event, True)
        return carry

    lax.fori_loop(0, 3, here, 0)
    lax.fori_loop(3, 2 * CHAIN - 1, later, 0)

    def y_copy(j):
        own = yb.at[j, mine, :]
        return remote(own, own, y_s.at[j], y_r.at[j], {"row": sib})

    turn(far_tile, occ - 1)

    def last_y(j, carry):
        right = tc[slot[(occ - 1) * occ + j], pl.ds(pl.multiple_of(far_tile * wide, wide), wide), :]
        yb[j, mine, :] = (acc[j] + times(piece_of(far_tile, occ - 1), right)).astype(BF16)
        y_copy(j).start()
        return carry

    lax.fori_loop(0, occ, last_y, 0)

    @pl.when(inner)
    def _():
        chols.sent(centre)
        amps.begin(centre)

    def turned_done(k, carry):
        turned(z, k).wait_send()
        for o in range(CHAIN):
            turned(o, k).wait_recv()
        return carry

    lax.fori_loop(0, occ, turned_done, 0)

    def side(first):
        return pl.ds(pl.multiple_of(first * half, half), half)

    def partial(q, j, first):
        return times(ct[q], yb[j, :, side(first)])

    def kept(first):
        return ybit + first * (xbit - ybit)

    def rs1(first, j, n):
        return remote(
            ss1.at[first, j % 2, n], rr1.at[first, j, n], rs1_s.at[first, j, n], rs1_r.at[first, j, n],
            {"row": along(first)},
        )

    def rs2(first, j):
        return remote(
            ss2.at[first, j % 2], rr2.at[first, j], rs2_s.at[first, j], rs2_r.at[first, j],
            {"row": along(1 - first)},
        )

    def scatter_one(j):
        y_copy(j).wait_recv()

        def each(step, carry):
            first, second = lax.rem(step, 2), step // 2
            n = kept(first) + (1 - second) * (1 - 2 * kept(first))
            q = (1 - first) * (2 * n + 1 - xbit) + first * (2 * (1 - ybit) + n)
            if j > 1:
                rs1(first, j - 2, n).wait_send()
            ss1[first, j % 2, n] = partial(q, j, first).astype(BF16)
            rs1(first, j, n).start()
            return carry

        lax.fori_loop(0, 4, each, 0)

    def scatter_two(j):
        def each(first, carry):
            other = 1 - kept(first)
            block = partial(along(1 - first) // 2, j, first)
            rs1(first, j, other).wait_recv()
            block += rr1[first, j, other].astype(F32)
            if j > 1:
                rs2(first, j - 2).wait_send()
            ss2[first, j % 2] = block.astype(BF16)
            rs2(first, j).start()
            return carry

        lax.fori_loop(0, 2, each, 0)

    def scatter_end(j):
        def each(first, carry):
            block = partial(chip, j, first)
            rs1(first, j, kept(first)).wait_recv()
            block += rr1[first, j, kept(first)].astype(F32)
            rs2(first, j).wait_recv()
            block += rr2[first, j].astype(F32)
            acc[j, :, side(first)] = block
            for k in range(occ):
                tc[j * occ + k, pl.ds(pl.multiple_of(me * size, size), size), side(first)] = (
                    block[k * size:(k + 1) * size].astype(BF16)
                )
            return carry

        lax.fori_loop(0, 2, each, 0)

    def gather_of(j):
        def view(low, count):
            return tc.at[j * occ:(j + 1) * occ, pl.ds(low, count), :]

        return Gather(view, lambda low, count: view(pl.multiple_of(me * size + low, 16), count), size, ag_s.at[j], ag_r.at[j])

    gathers = [gather_of(j) for j in range(occ)]

    def bring(dist, own=False):
        if own:
            copy = pltpu.make_async_copy(slabs_ref, cp.at[z], local.at[0])
            copy.start()
            copy.wait()
            return
        for way in (0, 1):
            @pl.when(amps.exists(way, dist))
            def _():
                def step(k, carry):
                    amps.arrive(way, dist, k)
                    return carry

                lax.fori_loop(0, occ, step, 0)
                origin = amps.origin(way, dist)
                copy = pltpu.make_async_copy(tr_ref.at[origin], cp.at[origin], local.at[0])
                copy.start()
                copy.wait()

    def add_r(origin, j):
        right = tc[pl.ds(j * occ, occ), pl.ds(pl.multiple_of(origin * wide, wide), wide), :].reshape(occ * wide, wide)
        for i in range(occ):
            left = jnp.concatenate([cp[origin, slot[i * occ + k]] for k in range(occ)], axis=1)
            acc[j, i * size:(i + 1) * size] += times(left, right)

    def product(low, high, first, last):
        def each(event, carry):
            dist, way = (event + 1) // 2, lax.rem(event + 1, 2)
            origin = chols.origin(way, dist)

            @pl.when(chols.exists(way, dist))
            def _():
                def step(n, inside):
                    add_r(origin, first + n)
                    return inside

                lax.fori_loop(0, last - first, step, 0)

            return carry

        lax.fori_loop(low, high, each, 0)

    far_chip = 2 * (1 - ybit) + (1 - xbit)
    late_tile = jnp.where(inner, CHAIN, far_tile)

    def product_where(j, near, soon):
        def each(o, carry):
            fits = (o != far_chip) if near else (o == far_chip)
            if soon is not None:
                fits = jnp.logical_and(fits, (o != late_tile) if soon else (o == late_tile))

            @pl.when(fits)
            def _():
                add_r(o, j)

            return carry

        lax.fori_loop(0, CHAIN, each, 0)

    def hand_out(j):
        return pltpu.make_async_copy(acc.at[j], r_ref.at[j], outs.at[j])

    scatter_one(0)
    scatter_one(1)
    scatter_two(0)
    scatter_one(2)
    scatter_two(1)
    scatter_end(0)
    gathers[0].begin()
    chols.sent(1 - centre)

    @pl.when(inner)
    def _():
        amps.begin(1 - centre)

    scatter_two(2)
    scatter_end(1)
    gathers[1].begin()
    bring(0, own=True)
    gathers[0].relay()
    scatter_end(2)
    gathers[2].begin()
    bring(1)
    gathers[1].relay()
    gathers[0].last()
    gathers[0].near()
    gathers[0].distant()
    product(0, 3, 0, 1)
    bring(2)
    product(3, 5, 0, 1)
    gathers[1].near()
    product_where(1, True, True)
    gathers[1].last()
    gathers[1].distant()
    gathers[2].relay()
    gathers[2].near()
    product_where(2, True, True)
    bring(3)
    product(5, 7, 0, 1)
    product_where(1, True, False)
    product_where(1, False, None)
    hand_out(0).start()
    hand_out(1).start()
    gathers[2].last()
    product_where(2, True, False)
    gathers[2].distant()
    product_where(2, False, None)
    hand_out(2).start()
    for j in range(occ):
        gathers[j].sent()
    for first in (0, 1):
        for j in (1, 2):
            for n in (0, 1):
                rs1(first, j, n).wait_send()
            rs2(first, j).wait_send()

    def y_done(j, carry):
        y_copy(j).wait_send()
        return carry

    lax.fori_loop(0, occ, y_done, 0)
    amps.sent(0)
    amps.sent(1)
    for j in range(occ):
        hand_out(j).wait()


def in_one_kernel(chol, amps, pairs):
    occ, depth, wide = chol.shape
    _, size, _ = amps.shape
    tall, full = occ * size, size * PLANE
    half = wide // 2
    dma = pltpu.SemaphoreType.DMA
    result, _ = pl.pallas_call(
        whole_kernel,
        out_shape=(
            jax.ShapeDtypeStruct((occ, tall, wide), F32),
            jax.ShapeDtypeStruct((CHAIN, occ * occ, size, wide), BF16),
        ),
        in_specs=[pl.BlockSpec(memory_space=pltpu.SMEM)] + [pl.BlockSpec(memory_space=pl.ANY)] * 2,
        out_specs=(pl.BlockSpec(memory_space=pl.ANY), pl.BlockSpec(memory_space=pl.ANY)),
        scratch_shapes=[
            pltpu.SMEM((occ * occ,), jnp.int32),
            pltpu.VMEM((CHAIN, occ * occ, size, wide), BF16),
            pltpu.VMEM((occ * occ, full, wide), BF16),
            pltpu.VMEM((CHAIN, tall, 2 * depth), BF16),
            pltpu.VMEM((occ, size, depth), BF16),
            pltpu.VMEM((occ, 2 * depth, wide), BF16),
            pltpu.VMEM((occ, tall, wide), F32),
            pltpu.VMEM((2, 2, 2, tall, half), BF16),
            pltpu.VMEM((2, occ, 2, tall, half), BF16),
            pltpu.VMEM((2, 2, tall, half), BF16),
            pltpu.VMEM((2, occ, tall, half), BF16),
            dma((2,)),
            dma((occ,)),
            dma((2, CHAIN - 1, occ)),
            dma((2, CHAIN - 1, occ)),
            dma((2, CHAIN - 1, occ)),
            dma((2, CHAIN - 1, occ)),
            dma((occ + 1, PIECES)),
            dma((occ + 1, PIECES)),
            dma((occ,)),
            dma((CHAIN, occ)),
            dma((occ,)),
            dma((occ,)),
            dma((2, occ, 2)),
            dma((2, occ, 2)),
            dma((2, occ)),
            dma((2, occ)),
        ],
        compiler_params=pltpu.CompilerParams(
            collective_id=0, has_side_effects=True, vmem_limit_bytes=62 * 1024 * 1024
        ),
        cost_estimate=pl.CostEstimate(
            flops=6 * occ * depth * occ * full * wide, bytes_accessed=32 * chol.size, transcendentals=0
        ),
        name="whole",
    )(pairs.T, chol.reshape(amps.shape), amps)
    return result.reshape(occ * occ, size, wide)


def in_steps(chol, amps, pairs):
    occ, depth, _ = chol.shape
    _, size, wide = amps.shape
    order = jnp.arange(occ * occ, dtype=jnp.int32)
    flat_pair = pairs[:, 0] * occ + pairs[:, 1]
    matches = (flat_pair[None, :] == order[:, None]).astype(jnp.int32)
    grid = jnp.take(amps, jnp.sum(matches * order[None, :], axis=1), axis=0, mode="clip")
    slabs = grid.reshape(occ, occ, size, wide)
    cols = lax.all_gather(slabs, "row", axis=2, tiled=True)
    chol_rows = lax.all_gather(chol, "col", axis=2, tiled=True)
    y = lax.dot_general(chol_rows, cols, (((0, 2), (0, 2)), ((), ())), preferred_element_type=F32)
    y = (y + jnp.transpose(chol, (1, 0, 2)).astype(F32)).astype(BF16)
    swapped = lax.all_to_all(chol_rows, "row", split_axis=2, concat_axis=1, tiled=True)
    y = lax.all_gather(y.reshape(depth, occ * wide), "row", axis=0, tiled=True)
    dressed = lax.dot_general(swapped, y, (((1,), (0,)), ((), ())), preferred_element_type=F32)
    dressed_cols = lax.all_gather(dressed.astype(BF16), "row", axis=1, tiled=True)
    rows = lax.all_gather(slabs, "col", axis=3, tiled=True)
    total = lax.dot_general(rows, dressed_cols, (((1, 3), (0, 1)), ((), ())), preferred_element_type=F32)
    total = (total + dressed).reshape(occ, size, occ, wide)
    return jnp.transpose(total, (2, 0, 1, 3)).reshape(occ * occ, size, wide)


def close_kernel(pairs_ref, levels_ref, vir_ref, r_ref, amp_ref, out_ref, base, r, amp, out, r_sem, amp_sem, out_sem):
    size, wide = base.shape
    occ = levels_ref.shape[0]
    slabs = r.shape[0]

    def load(s):
        index = pairs_ref[1, s] * occ + pairs_ref[0, s]
        return (
            pltpu.make_async_copy(r_ref.at[index], r.at[s], r_sem.at[s]),
            pltpu.make_async_copy(amp_ref.at[s], amp.at[s], amp_sem.at[s]),
        )

    def store(s):
        return pltpu.make_async_copy(out.at[s], out_ref.at[s], out_sem.at[s])

    for s in range(AHEAD):
        for copy in load(s):
            copy.start()
    rows = vir_ref[:, pl.ds(pl.multiple_of(lax.axis_index("row") * size, size), size)]
    cols = vir_ref[:, pl.ds(pl.multiple_of(lax.axis_index("col") * wide, wide), wide)]
    rows = jnp.transpose(jnp.broadcast_to(rows, (128, size)), (1, 0))
    base[...] = rows[:, :1] + cols

    def one(s, carry):
        @pl.when(s + AHEAD < slabs)
        def _():
            for copy in load(s + AHEAD):
                copy.start()

        for copy in load(s):
            copy.wait()
        levels = levels_ref[pairs_ref[0, s]] + levels_ref[pairs_ref[1, s]]
        out[s] = r[s] + (base[...] - levels) * amp[s].astype(F32)
        store(s).start()
        return carry

    lax.fori_loop(0, slabs, one, 0)
    for s in range(slabs):
        store(s).wait()


def close(product, amps, eps_occ, eps_vir, pairs):
    slabs, size, wide = amps.shape
    return pl.pallas_call(
        close_kernel,
        out_shape=jax.ShapeDtypeStruct(amps.shape, F32),
        in_specs=[
            pl.BlockSpec(memory_space=pltpu.SMEM),
            pl.BlockSpec(memory_space=pltpu.SMEM),
            pl.BlockSpec(memory_space=pltpu.VMEM),
            pl.BlockSpec(memory_space=pl.ANY),
            pl.BlockSpec(memory_space=pl.ANY),
        ],
        out_specs=pl.BlockSpec(memory_space=pl.ANY),
        scratch_shapes=[
            pltpu.VMEM((size, wide), F32),
            pltpu.VMEM(amps.shape, F32),
            pltpu.VMEM(amps.shape, BF16),
            pltpu.VMEM(amps.shape, F32),
            pltpu.SemaphoreType.DMA((slabs,)),
            pltpu.SemaphoreType.DMA((slabs,)),
            pltpu.SemaphoreType.DMA((slabs,)),
        ],
        compiler_params=pltpu.CompilerParams(vmem_limit_bytes=62 * 1024 * 1024),
        name="close",
    )(pairs.T, eps_occ, eps_vir.reshape(1, -1), product, amps)


def per_device(chol, amps, eps_occ, eps_vir, pairs):
    occ, depth, wide = chol.shape
    size = amps.shape[1]
    one = lax.axis_size("row") == PLANE and lax.axis_size("col") == CHAIN
    one = one and depth == occ * size and wide == 2 * size
    product = (in_one_kernel if one else in_steps)(chol, amps, pairs)
    return close(product, amps, eps_occ, eps_vir, pairs)


def solution(mesh):
    placed = (P(None, "row", "col"), P(None, "row", "col"), P(), P(), P())
    return jax.shard_map(
        per_device, mesh=mesh, in_specs=placed, out_specs=P(None, "row", "col"), check_vma=False
    )
```

```python
import functools

import jax
import jax.numpy as jnp
from jax import lax
from jax.experimental import pallas as pl
from jax.experimental.pallas import tpu as pltpu
from jax.sharding import PartitionSpec as P

F32 = jnp.float32
BF16 = jnp.bfloat16
MESH = pl.DeviceIdType.MESH
PLANE = 8
CHAIN = 4
PIECES = 11
AHEAD = 4


def remote(src, dst, send, recv, where):
    return pltpu.make_async_remote_copy(
        src_ref=src, dst_ref=dst, send_sem=send, recv_sem=recv, device_id=where, device_id_type=MESH
    )


def times(left, right):
    return jnp.dot(left, right, preferred_element_type=F32)


class Gather:
    def __init__(self, view, own, size, send, recv):
        me = lax.axis_index("row")
        core, xbit, ybit = lax.rem(me, 2), lax.rem(me // 2, 2), me // 4
        sib, xn, yn = me + 1 - 2 * core, me + 2 - 4 * xbit, me + 4 - 8 * ybit
        far = xn + 4 - 8 * ybit
        half = size // 2

        def part(origin, low, count):
            return view(pl.multiple_of(origin * size + low, 16), count)

        def make(index, src, dst, where):
            return remote(src, dst, send.at[index], recv.at[index], {"row": where})

        def hand_on(index, origin, low, count, where):
            return make(index, part(origin, low, count), part(origin, low, count), where)

        self.copies = [
            make(0, own(0, half), part(me, 0, half), xn),
            make(1, own(half, half), part(me, half, half), xn),
            make(2, own(half, half), part(me, half, half), yn),
            make(3, own(0, half), part(me, 0, half), yn),
            make(4, own(0, size), part(me, 0, size), sib),
            hand_on(5, xn, 0, half, yn),
            hand_on(6, yn, half, half, xn),
            hand_on(7, xn, 0, size, sib),
            hand_on(8, yn, 0, size, sib),
            hand_on(9, far, 0, half, sib),
            hand_on(10, far, half, half, sib),
        ]

    def begin(self):
        for index in (0, 2, 1, 3, 4):
            self.copies[index].start()

    def relay(self):
        for arrived, onward in ((0, 5), (2, 6), (1, 7), (3, 8)):
            self.copies[arrived].wait_recv()
            self.copies[onward].start()

    def last(self):
        for arrived, onward in ((5, 9), (6, 10)):
            self.copies[arrived].wait_recv()
            self.copies[onward].start()

    def near(self):
        for index in (4, 7, 8):
            self.copies[index].wait_recv()

    def distant(self):
        for index in (9, 10):
            self.copies[index].wait_recv()

    def sent(self):
        for copy in self.copies:
            copy.wait_send()


class Chain:
    def __init__(self, panel, own, count, send, recv):
        self.panel, self.own, self.count, self.send, self.recv = panel, own, count, send, recv
        self.z = lax.axis_index("col")

    def piece(self, k):
        return pl.ds(k * self.count, self.count)

    def origin(self, way, dist):
        return self.z + dist * (1 - 2 * way)

    def exists(self, way, dist):
        origin = self.origin(way, dist)
        return jnp.logical_and(origin >= 0, origin < CHAIN)

    def onward(self, way):
        return self.exists(1 - way, 1)

    def hop(self, way, dist, k, own=False):
        origin = self.z if own else self.origin(way, dist - 1)
        src = self.own.at[self.piece(k)] if own else self.panel.at[origin, self.piece(k)]
        where = {"col": self.z - 1 + 2 * way}
        return remote(
            src, self.panel.at[origin, self.piece(k)], self.send.at[way, dist - 1, k], self.recv.at[way, dist - 1, k], where
        )

    def begin(self, way):
        @pl.when(self.onward(way))
        def _():
            for k in range(self.count):
                self.hop(way, 1, k, own=True).start()

    def arrive(self, way, dist, k):
        origin = self.origin(way, dist)
        sem = (way, dist - 1, k)
        remote(
            self.panel.at[origin, self.piece(k)], self.panel.at[origin, self.piece(k)],
            self.send.at[sem], self.recv.at[sem], {"col": origin},
        ).wait_recv()

        @pl.when(self.onward(way))
        def _():
            self.hop(way, dist + 1, k).start()

    def sent(self, way):
        for dist in range(1, CHAIN):
            @pl.when(jnp.logical_and(self.onward(way), self.exists(way, dist - 1)))
            def _():
                for k in range(self.count):
                    self.hop(way, dist, k, own=dist == 1).wait_send()


def whole_kernel(
    pairs_ref, chol_ref, slabs_ref, r_ref, tr_ref,
    slot, cp, tc, ct, cts, yb, acc, ss1, rr1, ss2, rr2,
    local, outs, cz_s, cz_r, tz_s, tz_r, ag_s, ag_r, ct_s, ct_r, y_s, y_r, rs1_s, rs1_r, rs2_s, rs2_r,
):
    occ = r_ref.shape[0]
    _, size, wide = slabs_ref.shape
    depth = tall = occ * size
    half = wide // 2
    me, z = lax.axis_index("row"), lax.axis_index("col")
    core, chip = lax.rem(me, 2), me // 2
    xbit, ybit = lax.rem(chip, 2), chip // 2
    sib, xn, yn = me + 1 - 2 * core, me + 2 - 4 * xbit, me + 4 - 8 * ybit
    inner = jnp.logical_and(z > 0, z < CHAIN - 1)
    centre = 1 - (2 * z) // CHAIN

    def along(first):
        return xn + first * (yn - xn)

    barrier = pltpu.get_barrier_semaphore()

    def greet(where):
        pl.semaphore_signal(barrier, inc=1, device_id=where, device_id_type=MESH)

    for row in (sib, xn, yn):
        greet({"row": row})

    @pl.when(z > 0)
    def _():
        greet({"col": z - 1})

    @pl.when(z < CHAIN - 1)
    def _():
        greet({"col": z + 1})

    @pl.when(inner)
    def _():
        pl.semaphore_wait(barrier, 5)

    @pl.when(jnp.logical_not(inner))
    def _():
        pl.semaphore_wait(barrier, 4)

    chols = Chain(cp, chol_ref, occ, cz_s, cz_r)
    amps = Chain(tr_ref, slabs_ref, occ, tz_s, tz_r)
    cols = Gather(
        lambda low, count: tc.at[:, pl.ds(low, count), :],
        lambda low, count: slabs_ref.at[:, pl.ds(low, count), :],
        size, ag_s.at[occ], ag_r.at[occ],
    )
    chols.begin(0)
    chols.begin(1)
    cols.begin()
    keep_c = pltpu.make_async_copy(chol_ref, cp.at[z], local.at[0])
    keep_t = pltpu.make_async_copy(
        slabs_ref, tc.at[:, pl.ds(pl.multiple_of(me * size, size), size), :], local.at[1]
    )
    keep_c.start()
    keep_t.start()
    for pair in range(occ * occ):
        found = jnp.int32(0)
        for s in range(occ * occ):
            same = pairs_ref[0, s] * occ + pairs_ref[1, s] == pair
            found += s * same.astype(jnp.int32)
        slot[pair] = jnp.minimum(found, occ * occ - 1)
    keep_c.wait()
    keep_t.wait()

    def near(k, carry):
        for way in (0, 1):
            @pl.when(chols.exists(way, 1))
            def _():
                chols.arrive(way, 1, k)
        return carry

    lax.fori_loop(0, occ, near, 0)
    cols.relay()

    def piece_of(o, k):
        return cp[o, pl.ds(k * occ, occ)].reshape(depth, wide)

    def first_y(j, carry):
        acc[j] = piece_of(z, j).astype(F32)
        return carry

    lax.fori_loop(0, occ, first_y, 0)
    cols.last()
    cols.near()
    cols.distant()
    cols.sent()

    @pl.when(jnp.logical_not(inner))
    def _():
        chols.sent(centre)
        amps.begin(centre)

    mine = pl.ds(pl.multiple_of(core * depth, depth), depth)

    def turned(o, k):
        return remote(
            cts.at[k], ct.at[o, pl.ds(pl.multiple_of(k * size, size), size), mine],
            ct_s.at[k], ct_r.at[o, k], {"row": sib},
        )

    def turn(o, k):
        def half_of(which):
            block = cp[o, pl.ds(k * occ, occ), :, pl.ds(pl.multiple_of(which * size, size), size)]
            return jnp.transpose(block.reshape(depth, size), (1, 0))

        cts[k] = half_of(1 - core)
        turned(o, k).start()
        ct[o, pl.ds(pl.multiple_of(k * size, size), size), mine] = half_of(core)

    def add_y(o, k):
        def one(j, carry):
            acc[j] += times(piece_of(o, k), tc[slot[k * occ + j], pl.ds(pl.multiple_of(o * wide, wide), wide), :])
            return carry

        lax.fori_loop(0, occ, one, 0)

    far_dist = jnp.where(inner, CHAIN // 2, CHAIN - 1)
    far_tile = chols.origin(1 - centre, far_dist)

    def come(event, waiting):
        dist, way = (event + 1) // 2, lax.rem(event + 1, 2)
        origin = chols.origin(way, dist)

        @pl.when(chols.exists(way, dist))
        def _():
            def step(k, carry):
                if waiting:
                    chols.arrive(way, dist, k)

                @pl.when(event > 0)
                def _():
                    turned(origin, k).wait_send()

                if waiting:
                    @pl.when(jnp.logical_or(origin != far_tile, k < occ - 1))
                    def _():
                        turn(origin, k)
                        add_y(origin, k)
                else:
                    turn(origin, k)
                    add_y(origin, k)
                return carry

            lax.fori_loop(0, occ, step, 0)

    def here(event, carry):
        come(event, False)
        return carry

    def later(event, carry):
        come(event, True)
        return carry

    lax.fori_loop(0, 3, here, 0)
    lax.fori_loop(3, 2 * CHAIN - 1, later, 0)

    def side(first):
        return pl.ds(pl.multiple_of(first * half, half), half)

    def y_copy(j, first):
        own = yb.at[j, mine, side(first)]
        return remote(own, own, y_s.at[j, first], y_r.at[j, first], {"row": sib})

    turn(far_tile, occ - 1)

    def last_y(n, carry):
        j, first = n // 2, lax.rem(n, 2)
        rows = pl.ds(pl.multiple_of(far_tile * wide, wide), wide)
        right = tc[slot[(occ - 1) * occ + j], rows, side(first)]
        total = acc[j, :, side(first)] + times(piece_of(far_tile, occ - 1), right)
        yb[j, mine, side(first)] = total.astype(BF16)
        y_copy(j, first).start()
        return carry

    lax.fori_loop(0, 2 * occ, last_y, 0)

    @pl.when(inner)
    def _():
        chols.sent(centre)
        amps.begin(centre)

    def turned_done(k, carry):
        turned(z, k).wait_send()
        for o in range(CHAIN):
            turned(o, k).wait_recv()
        return carry

    lax.fori_loop(0, occ, turned_done, 0)

    def partial(q, j, first):
        return times(ct[q], yb[j, :, side(first)])

    def kept(first):
        return ybit + first * (xbit - ybit)

    def rs1(first, j, n):
        return remote(
            ss1.at[first, j % 2, n], rr1.at[first, j, n], rs1_s.at[first, j, n], rs1_r.at[first, j, n],
            {"row": along(first)},
        )

    def rs2(first, j):
        return remote(
            ss2.at[first, j % 2], rr2.at[first, j], rs2_s.at[first, j], rs2_r.at[first, j],
            {"row": along(1 - first)},
        )

    def scatter_one(j):
        def each(step, carry):
            first, second = lax.rem(step, 2), step // 2

            @pl.when(second == 0)
            def _():
                y_copy(j, first).wait_recv()

            n = kept(first) + (1 - second) * (1 - 2 * kept(first))
            q = (1 - first) * (2 * n + 1 - xbit) + first * (2 * (1 - ybit) + n)
            if j > 1:
                rs1(first, j - 2, n).wait_send()
            ss1[first, j % 2, n] = partial(q, j, first).astype(BF16)
            rs1(first, j, n).start()
            return carry

        lax.fori_loop(0, 4, each, 0)

    def scatter_two(j):
        def each(first, carry):
            other = 1 - kept(first)
            block = partial(along(1 - first) // 2, j, first)
            rs1(first, j, other).wait_recv()
            block += rr1[first, j, other].astype(F32)
            if j > 1:
                rs2(first, j - 2).wait_send()
            ss2[first, j % 2] = block.astype(BF16)
            rs2(first, j).start()
            return carry

        lax.fori_loop(0, 2, each, 0)

    def scatter_end(j):
        def each(first, carry):
            block = partial(chip, j, first)
            rs1(first, j, kept(first)).wait_recv()
            block += rr1[first, j, kept(first)].astype(F32)
            rs2(first, j).wait_recv()
            block += rr2[first, j].astype(F32)
            acc[j, :, side(first)] = block
            for k in range(occ):
                tc[j * occ + k, pl.ds(pl.multiple_of(me * size, size), size), side(first)] = (
                    block[k * size:(k + 1) * size].astype(BF16)
                )
            return carry

        lax.fori_loop(0, 2, each, 0)

    def gather_of(j):
        def view(low, count):
            return tc.at[j * occ:(j + 1) * occ, pl.ds(low, count), :]

        return Gather(view, lambda low, count: view(pl.multiple_of(me * size + low, 16), count), size, ag_s.at[j], ag_r.at[j])

    gathers = [gather_of(j) for j in range(occ)]

    def bring(dist, own=False):
        if own:
            copy = pltpu.make_async_copy(slabs_ref, cp.at[z], local.at[0])
            copy.start()
            copy.wait()
            return
        for way in (0, 1):
            @pl.when(amps.exists(way, dist))
            def _():
                def step(k, carry):
                    amps.arrive(way, dist, k)
                    return carry

                lax.fori_loop(0, occ, step, 0)
                origin = amps.origin(way, dist)
                copy = pltpu.make_async_copy(tr_ref.at[origin], cp.at[origin], local.at[0])
                copy.start()
                copy.wait()

    def add_r(origin, j):
        right = tc[pl.ds(j * occ, occ), pl.ds(pl.multiple_of(origin * wide, wide), wide), :].reshape(occ * wide, wide)
        for i in range(occ):
            left = jnp.concatenate([cp[origin, slot[i * occ + k]] for k in range(occ)], axis=1)
            acc[j, i * size:(i + 1) * size] += times(left, right)

    def product(low, high, first, last):
        def each(event, carry):
            dist, way = (event + 1) // 2, lax.rem(event + 1, 2)
            origin = chols.origin(way, dist)

            @pl.when(chols.exists(way, dist))
            def _():
                def step(n, inside):
                    add_r(origin, first + n)
                    return inside

                lax.fori_loop(0, last - first, step, 0)

            return carry

        lax.fori_loop(low, high, each, 0)

    far_chip = 2 * (1 - ybit) + (1 - xbit)
    late_tile = jnp.where(inner, CHAIN, far_tile)

    def product_where(j, near, soon):
        def each(o, carry):
            fits = (o != far_chip) if near else (o == far_chip)
            if soon is not None:
                fits = jnp.logical_and(fits, (o != late_tile) if soon else (o == late_tile))

            @pl.when(fits)
            def _():
                add_r(o, j)

            return carry

        lax.fori_loop(0, CHAIN, each, 0)

    def hand_out(j, i):
        rows = pl.ds(i * size, size)
        return pltpu.make_async_copy(acc.at[j, rows], r_ref.at[j, rows], outs.at[j, i])

    def add_far(j):
        start = far_chip * wide
        near_rows = pl.ds(pl.multiple_of(start + core * size, size), size)
        sib_rows = pl.ds(pl.multiple_of(start + (1 - core) * size, size), size)

        def part(i, rows, which):
            right = tc[j * occ:(j + 1) * occ, rows, :].reshape(tall, wide)
            columns = pl.ds(pl.multiple_of(which * size, size), size)
            left = jnp.concatenate([cp[far_chip, slot[i * occ + k], :, columns] for k in range(occ)], axis=1)
            acc[j, i * size:(i + 1) * size] += times(left, right)

        for i in range(occ):
            part(i, near_rows, core)
        gathers[j].distant()
        for i in range(occ):
            part(i, sib_rows, 1 - core)
            hand_out(j, i).start()

    scatter_one(0)
    scatter_one(1)
    scatter_two(0)
    scatter_one(2)
    scatter_two(1)
    scatter_end(0)
    gathers[0].begin()
    chols.sent(1 - centre)

    @pl.when(inner)
    def _():
        amps.begin(1 - centre)

    scatter_two(2)
    scatter_end(1)
    gathers[1].begin()
    bring(0, own=True)
    gathers[0].relay()
    scatter_end(2)
    gathers[2].begin()
    bring(1)
    gathers[1].relay()
    gathers[0].last()
    gathers[0].near()
    gathers[0].distant()
    product(0, 3, 0, 1)
    bring(2)
    product(3, 5, 0, 1)
    gathers[1].near()
    product_where(1, True, True)
    gathers[1].last()
    gathers[1].distant()
    gathers[2].relay()
    gathers[2].near()
    product_where(2, True, True)
    bring(3)
    product(5, 7, 0, 1)
    product_where(1, True, False)
    product_where(1, False, None)
    for i in range(occ):
        hand_out(0, i).start()
        hand_out(1, i).start()
    gathers[2].last()
    product_where(2, True, False)
    add_far(2)
    for j in range(occ):
        gathers[j].sent()
    for first in (0, 1):
        for j in (1, 2):
            for n in (0, 1):
                rs1(first, j, n).wait_send()
            rs2(first, j).wait_send()

    def y_done(j, carry):
        for first in (0, 1):
            y_copy(j, first).wait_send()
        return carry

    lax.fori_loop(0, occ, y_done, 0)
    amps.sent(0)
    amps.sent(1)
    for j in range(occ):
        for i in range(occ):
            hand_out(j, i).wait()


def in_one_kernel(chol, amps, pairs):
    occ, depth, wide = chol.shape
    _, size, _ = amps.shape
    tall, full = occ * size, size * PLANE
    half = wide // 2
    dma = pltpu.SemaphoreType.DMA
    result, _ = pl.pallas_call(
        whole_kernel,
        out_shape=(
            jax.ShapeDtypeStruct((occ, tall, wide), F32),
            jax.ShapeDtypeStruct((CHAIN, occ * occ, size, wide), BF16),
        ),
        in_specs=[pl.BlockSpec(memory_space=pltpu.SMEM)] + [pl.BlockSpec(memory_space=pl.ANY)] * 2,
        out_specs=(pl.BlockSpec(memory_space=pl.ANY), pl.BlockSpec(memory_space=pl.ANY)),
        scratch_shapes=[
            pltpu.SMEM((occ * occ,), jnp.int32),
            pltpu.VMEM((CHAIN, occ * occ, size, wide), BF16),
            pltpu.VMEM((occ * occ, full, wide), BF16),
            pltpu.VMEM((CHAIN, tall, 2 * depth), BF16),
            pltpu.VMEM((occ, size, depth), BF16),
            pltpu.VMEM((occ, 2 * depth, wide), BF16),
            pltpu.VMEM((occ, tall, wide), F32),
            pltpu.VMEM((2, 2, 2, tall, half), BF16),
            pltpu.VMEM((2, occ, 2, tall, half), BF16),
            pltpu.VMEM((2, 2, tall, half), BF16),
            pltpu.VMEM((2, occ, tall, half), BF16),
            dma((2,)),
            dma((occ, occ)),
            dma((2, CHAIN - 1, occ)),
            dma((2, CHAIN - 1, occ)),
            dma((2, CHAIN - 1, occ)),
            dma((2, CHAIN - 1, occ)),
            dma((occ + 1, PIECES)),
            dma((occ + 1, PIECES)),
            dma((occ,)),
            dma((CHAIN, occ)),
            dma((occ, 2)),
            dma((occ, 2)),
            dma((2, occ, 2)),
            dma((2, occ, 2)),
            dma((2, occ)),
            dma((2, occ)),
        ],
        compiler_params=pltpu.CompilerParams(
            collective_id=0, has_side_effects=True, vmem_limit_bytes=62 * 1024 * 1024
        ),
        cost_estimate=pl.CostEstimate(
            flops=6 * occ * depth * occ * full * wide, bytes_accessed=32 * chol.size, transcendentals=0
        ),
        name="whole",
    )(pairs.T, chol.reshape(amps.shape), amps)
    return result.reshape(occ * occ, size, wide)


def in_steps(chol, amps, pairs):
    occ, depth, _ = chol.shape
    _, size, wide = amps.shape
    order = jnp.arange(occ * occ, dtype=jnp.int32)
    flat_pair = pairs[:, 0] * occ + pairs[:, 1]
    matches = (flat_pair[None, :] == order[:, None]).astype(jnp.int32)
    grid = jnp.take(amps, jnp.sum(matches * order[None, :], axis=1), axis=0, mode="clip")
    slabs = grid.reshape(occ, occ, size, wide)
    cols = lax.all_gather(slabs, "row", axis=2, tiled=True)
    chol_rows = lax.all_gather(chol, "col", axis=2, tiled=True)
    y = lax.dot_general(chol_rows, cols, (((0, 2), (0, 2)), ((), ())), preferred_element_type=F32)
    y = (y + jnp.transpose(chol, (1, 0, 2)).astype(F32)).astype(BF16)
    swapped = lax.all_to_all(chol_rows, "row", split_axis=2, concat_axis=1, tiled=True)
    y = lax.all_gather(y.reshape(depth, occ * wide), "row", axis=0, tiled=True)
    dressed = lax.dot_general(swapped, y, (((1,), (0,)), ((), ())), preferred_element_type=F32)
    dressed_cols = lax.all_gather(dressed.astype(BF16), "row", axis=1, tiled=True)
    rows = lax.all_gather(slabs, "col", axis=3, tiled=True)
    total = lax.dot_general(rows, dressed_cols, (((1, 3), (0, 1)), ((), ())), preferred_element_type=F32)
    total = (total + dressed).reshape(occ, size, occ, wide)
    return jnp.transpose(total, (2, 0, 1, 3)).reshape(occ * occ, size, wide)


def close_kernel(pairs_ref, levels_ref, vir_ref, r_ref, amp_ref, out_ref, base, r, amp, out, r_sem, amp_sem, out_sem):
    size, wide = base.shape
    occ = levels_ref.shape[0]
    slabs = r.shape[0]

    def load(s):
        index = pairs_ref[1, s] * occ + pairs_ref[0, s]
        return (
            pltpu.make_async_copy(r_ref.at[index], r.at[s], r_sem.at[s]),
            pltpu.make_async_copy(amp_ref.at[s], amp.at[s], amp_sem.at[s]),
        )

    def store(s):
        return pltpu.make_async_copy(out.at[s], out_ref.at[s], out_sem.at[s])

    for s in range(AHEAD):
        for copy in load(s):
            copy.start()
    rows = vir_ref[:, pl.ds(pl.multiple_of(lax.axis_index("row") * size, size), size)]
    cols = vir_ref[:, pl.ds(pl.multiple_of(lax.axis_index("col") * wide, wide), wide)]
    rows = jnp.transpose(jnp.broadcast_to(rows, (128, size)), (1, 0))
    base[...] = rows[:, :1] + cols

    def one(s, carry):
        @pl.when(s + AHEAD < slabs)
        def _():
            for copy in load(s + AHEAD):
                copy.start()

        for copy in load(s):
            copy.wait()
        levels = levels_ref[pairs_ref[0, s]] + levels_ref[pairs_ref[1, s]]
        out[s] = r[s] + (base[...] - levels) * amp[s].astype(F32)
        store(s).start()
        return carry

    lax.fori_loop(0, slabs, one, 0)
    for s in range(slabs):
        store(s).wait()


def close(product, amps, eps_occ, eps_vir, pairs):
    slabs, size, wide = amps.shape
    return pl.pallas_call(
        close_kernel,
        out_shape=jax.ShapeDtypeStruct(amps.shape, F32),
        in_specs=[
            pl.BlockSpec(memory_space=pltpu.SMEM),
            pl.BlockSpec(memory_space=pltpu.SMEM),
            pl.BlockSpec(memory_space=pltpu.VMEM),
            pl.BlockSpec(memory_space=pl.ANY),
            pl.BlockSpec(memory_space=pl.ANY),
        ],
        out_specs=pl.BlockSpec(memory_space=pl.ANY),
        scratch_shapes=[
            pltpu.VMEM((size, wide), F32),
            pltpu.VMEM(amps.shape, F32),
            pltpu.VMEM(amps.shape, BF16),
            pltpu.VMEM(amps.shape, F32),
            pltpu.SemaphoreType.DMA((slabs,)),
            pltpu.SemaphoreType.DMA((slabs,)),
            pltpu.SemaphoreType.DMA((slabs,)),
        ],
        compiler_params=pltpu.CompilerParams(vmem_limit_bytes=62 * 1024 * 1024),
        name="close",
    )(pairs.T, eps_occ, eps_vir.reshape(1, -1), product, amps)


def per_device(chol, amps, eps_occ, eps_vir, pairs):
    occ, depth, wide = chol.shape
    size = amps.shape[1]
    one = lax.axis_size("row") == PLANE and lax.axis_size("col") == CHAIN
    one = one and depth == occ * size and wide == 2 * size
    product = (in_one_kernel if one else in_steps)(chol, amps, pairs)
    return close(product, amps, eps_occ, eps_vir, pairs)


def solution(mesh):
    placed = (P(None, "row", "col"), P(None, "row", "col"), P(), P(), P())
    return jax.shard_map(
        per_device, mesh=mesh, in_specs=placed, out_specs=P(None, "row", "col"), check_vma=False
    )
```

```python
import functools

import jax
import jax.numpy as jnp
from jax import lax
from jax.experimental import pallas as pl
from jax.experimental.pallas import tpu as pltpu
from jax.sharding import PartitionSpec as P

F32 = jnp.float32
BF16 = jnp.bfloat16
MESH = pl.DeviceIdType.MESH
PLANE = 8
CHAIN = 4
PIECES = 11
AHEAD = 4


def remote(src, dst, send, recv, where):
    return pltpu.make_async_remote_copy(
        src_ref=src, dst_ref=dst, send_sem=send, recv_sem=recv, device_id=where, device_id_type=MESH
    )


def times(left, right):
    return jnp.dot(left, right, preferred_element_type=F32)


class Gather:
    def __init__(self, view, own, size, send, recv):
        me = lax.axis_index("row")
        core, xbit, ybit = lax.rem(me, 2), lax.rem(me // 2, 2), me // 4
        sib, xn, yn = me + 1 - 2 * core, me + 2 - 4 * xbit, me + 4 - 8 * ybit
        far = xn + 4 - 8 * ybit
        half = size // 2

        def part(origin, low, count):
            return view(pl.multiple_of(origin * size + low, 16), count)

        def make(index, src, dst, where):
            return remote(src, dst, send.at[index], recv.at[index], {"row": where})

        def hand_on(index, origin, low, count, where):
            return make(index, part(origin, low, count), part(origin, low, count), where)

        self.copies = [
            make(0, own(0, half), part(me, 0, half), xn),
            make(1, own(half, half), part(me, half, half), xn),
            make(2, own(half, half), part(me, half, half), yn),
            make(3, own(0, half), part(me, 0, half), yn),
            make(4, own(0, size), part(me, 0, size), sib),
            hand_on(5, xn, 0, half, yn),
            hand_on(6, yn, half, half, xn),
            hand_on(7, xn, 0, size, sib),
            hand_on(8, yn, 0, size, sib),
            hand_on(9, far, 0, half, sib),
            hand_on(10, far, half, half, sib),
        ]

    def begin(self):
        for index in (0, 2, 1, 3, 4):
            self.copies[index].start()

    def relay(self):
        for arrived, onward in ((0, 5), (2, 6), (1, 7), (3, 8)):
            self.copies[arrived].wait_recv()
            self.copies[onward].start()

    def last(self):
        for arrived, onward in ((5, 9), (6, 10)):
            self.copies[arrived].wait_recv()
            self.copies[onward].start()

    def near(self):
        for index in (4, 7, 8):
            self.copies[index].wait_recv()

    def distant(self):
        for index in (9, 10):
            self.copies[index].wait_recv()

    def sent(self):
        for copy in self.copies:
            copy.wait_send()


class Chain:
    def __init__(self, panel, own, count, send, recv):
        self.panel, self.own, self.count, self.send, self.recv = panel, own, count, send, recv
        self.z = lax.axis_index("col")

    def piece(self, k):
        return pl.ds(k * self.count, self.count)

    def origin(self, way, dist):
        return self.z + dist * (1 - 2 * way)

    def exists(self, way, dist):
        origin = self.origin(way, dist)
        return jnp.logical_and(origin >= 0, origin < CHAIN)

    def onward(self, way):
        return self.exists(1 - way, 1)

    def hop(self, way, dist, k, own=False):
        origin = self.z if own else self.origin(way, dist - 1)
        src = self.own.at[self.piece(k)] if own else self.panel.at[origin, self.piece(k)]
        where = {"col": self.z - 1 + 2 * way}
        return remote(
            src, self.panel.at[origin, self.piece(k)], self.send.at[way, dist - 1, k], self.recv.at[way, dist - 1, k], where
        )

    def begin(self, way):
        @pl.when(self.onward(way))
        def _():
            for k in range(self.count):
                self.hop(way, 1, k, own=True).start()

    def arrive(self, way, dist, k):
        origin = self.origin(way, dist)
        sem = (way, dist - 1, k)
        remote(
            self.panel.at[origin, self.piece(k)], self.panel.at[origin, self.piece(k)],
            self.send.at[sem], self.recv.at[sem], {"col": origin},
        ).wait_recv()

        @pl.when(self.onward(way))
        def _():
            self.hop(way, dist + 1, k).start()

    def sent(self, way):
        for dist in range(1, CHAIN):
            @pl.when(jnp.logical_and(self.onward(way), self.exists(way, dist - 1)))
            def _():
                for k in range(self.count):
                    self.hop(way, dist, k, own=dist == 1).wait_send()


def whole_kernel(
    pairs_ref, chol_ref, slabs_ref, r_ref, tr_ref,
    slot, cp, tc, ct, cts, yb, acc, ss1, rr1, ss2, rr2,
    local, outs, cz_s, cz_r, tz_s, tz_r, ag_s, ag_r, ct_s, ct_r, y_s, y_r, rs1_s, rs1_r, rs2_s, rs2_r,
):
    occ = r_ref.shape[0]
    _, size, wide = slabs_ref.shape
    depth = tall = occ * size
    half = wide // 2
    me, z = lax.axis_index("row"), lax.axis_index("col")
    core, chip = lax.rem(me, 2), me // 2
    xbit, ybit = lax.rem(chip, 2), chip // 2
    sib, xn, yn = me + 1 - 2 * core, me + 2 - 4 * xbit, me + 4 - 8 * ybit
    inner = jnp.logical_and(z > 0, z < CHAIN - 1)
    centre = 1 - (2 * z) // CHAIN

    def along(first):
        return xn + first * (yn - xn)

    barrier = pltpu.get_barrier_semaphore()

    def greet(where):
        pl.semaphore_signal(barrier, inc=1, device_id=where, device_id_type=MESH)

    for row in (sib, xn, yn):
        greet({"row": row})

    @pl.when(z > 0)
    def _():
        greet({"col": z - 1})

    @pl.when(z < CHAIN - 1)
    def _():
        greet({"col": z + 1})

    @pl.when(inner)
    def _():
        pl.semaphore_wait(barrier, 5)

    @pl.when(jnp.logical_not(inner))
    def _():
        pl.semaphore_wait(barrier, 4)

    chols = Chain(cp, chol_ref, occ, cz_s, cz_r)
    amps = Chain(tr_ref, slabs_ref, occ, tz_s, tz_r)
    cols = Gather(
        lambda low, count: tc.at[:, pl.ds(low, count), :],
        lambda low, count: slabs_ref.at[:, pl.ds(low, count), :],
        size, ag_s.at[occ], ag_r.at[occ],
    )
    chols.begin(0)
    chols.begin(1)
    cols.begin()
    keep_c = pltpu.make_async_copy(chol_ref, cp.at[z], local.at[0])
    keep_t = pltpu.make_async_copy(
        slabs_ref, tc.at[:, pl.ds(pl.multiple_of(me * size, size), size), :], local.at[1]
    )
    keep_c.start()
    keep_t.start()
    for pair in range(occ * occ):
        found = jnp.int32(0)
        for s in range(occ * occ):
            same = pairs_ref[0, s] * occ + pairs_ref[1, s] == pair
            found += s * same.astype(jnp.int32)
        slot[pair] = jnp.minimum(found, occ * occ - 1)
    keep_c.wait()
    keep_t.wait()

    def near(k, carry):
        for way in (0, 1):
            @pl.when(chols.exists(way, 1))
            def _():
                chols.arrive(way, 1, k)
        return carry

    lax.fori_loop(0, occ, near, 0)
    cols.relay()

    def piece_of(o, k):
        return cp[o, pl.ds(k * occ, occ)].reshape(depth, wide)

    def first_y(j, carry):
        acc[j] = piece_of(z, j).astype(F32)
        return carry

    lax.fori_loop(0, occ, first_y, 0)
    cols.last()
    cols.near()
    cols.distant()
    cols.sent()

    @pl.when(jnp.logical_not(inner))
    def _():
        chols.sent(centre)
        amps.begin(centre)

    mine = pl.ds(pl.multiple_of(core * depth, depth), depth)

    def turned(o, k):
        return remote(
            cts.at[k], ct.at[o, pl.ds(pl.multiple_of(k * size, size), size), mine],
            ct_s.at[k], ct_r.at[o, k], {"row": sib},
        )

    def turn(o, k):
        def half_of(which):
            block = cp[o, pl.ds(k * occ, occ), :, pl.ds(pl.multiple_of(which * size, size), size)]
            return jnp.transpose(block.reshape(depth, size), (1, 0))

        cts[k] = half_of(1 - core)
        turned(o, k).start()
        ct[o, pl.ds(pl.multiple_of(k * size, size), size), mine] = half_of(core)

    def add_y(o, k):
        def one(j, carry):
            acc[j] += times(piece_of(o, k), tc[slot[k * occ + j], pl.ds(pl.multiple_of(o * wide, wide), wide), :])
            return carry

        lax.fori_loop(0, occ, one, 0)

    far_dist = jnp.where(inner, CHAIN // 2, CHAIN - 1)
    far_tile = chols.origin(1 - centre, far_dist)

    def come(event, waiting):
        dist, way = (event + 1) // 2, lax.rem(event + 1, 2)
        origin = chols.origin(way, dist)

        @pl.when(chols.exists(way, dist))
        def _():
            def step(k, carry):
                if waiting:
                    chols.arrive(way, dist, k)

                @pl.when(event > 0)
                def _():
                    turned(origin, k).wait_send()

                if waiting:
                    @pl.when(jnp.logical_or(origin != far_tile, k < occ - 1))
                    def _():
                        turn(origin, k)
                        add_y(origin, k)
                else:
                    turn(origin, k)
                    add_y(origin, k)
                return carry

            lax.fori_loop(0, occ, step, 0)

    def here(event, carry):
        come(event, False)
        return carry

    def later(event, carry):
        come(event, True)
        return carry

    lax.fori_loop(0, 3, here, 0)
    lax.fori_loop(3, 2 * CHAIN - 1, later, 0)

    def side(first):
        return pl.ds(pl.multiple_of(first * half, half), half)

    def y_copy(j, first):
        own = yb.at[j, mine, side(first)]
        return remote(own, own, y_s.at[j, first], y_r.at[j, first], {"row": sib})

    turn(far_tile, occ - 1)

    def last_y(n, carry):
        j, first = n // 2, lax.rem(n, 2)
        rows = pl.ds(pl.multiple_of(far_tile * wide, wide), wide)
        right = tc[slot[(occ - 1) * occ + j], rows, side(first)]
        total = acc[j, :, side(first)] + times(piece_of(far_tile, occ - 1), right)
        yb[j, mine, side(first)] = total.astype(BF16)
        y_copy(j, first).start()
        return carry

    lax.fori_loop(0, 2 * occ, last_y, 0)

    @pl.when(inner)
    def _():
        chols.sent(centre)
        amps.begin(centre)

    def turned_done(k, carry):
        turned(z, k).wait_send()
        for o in range(CHAIN):
            turned(o, k).wait_recv()
        return carry

    lax.fori_loop(0, occ, turned_done, 0)

    def partial(q, j, first):
        return times(ct[q], yb[j, :, side(first)])

    def kept(first):
        return ybit + first * (xbit - ybit)

    def rs1(first, j, n):
        return remote(
            ss1.at[first, j % 2, n], rr1.at[first, j, n], rs1_s.at[first, j, n], rs1_r.at[first, j, n],
            {"row": along(first)},
        )

    def rs2(first, j):
        return remote(
            ss2.at[first, j % 2], rr2.at[first, j], rs2_s.at[first, j], rs2_r.at[first, j],
            {"row": along(1 - first)},
        )

    def scatter_one(j):
        def each(step, carry):
            first, second = lax.rem(step, 2), step // 2

            @pl.when(second == 0)
            def _():
                y_copy(j, first).wait_recv()

            n = kept(first) + (1 - second) * (1 - 2 * kept(first))
            q = (1 - first) * (2 * n + 1 - xbit) + first * (2 * (1 - ybit) + n)
            if j > 1:
                rs1(first, j - 2, n).wait_send()
            ss1[first, j % 2, n] = partial(q, j, first).astype(BF16)
            rs1(first, j, n).start()
            return carry

        lax.fori_loop(0, 4, each, 0)

    def scatter_two(j):
        def each(first, carry):
            other = 1 - kept(first)
            block = partial(along(1 - first) // 2, j, first)
            rs1(first, j, other).wait_recv()
            block += rr1[first, j, other].astype(F32)
            if j > 1:
                rs2(first, j - 2).wait_send()
            ss2[first, j % 2] = block.astype(BF16)
            rs2(first, j).start()
            return carry

        lax.fori_loop(0, 2, each, 0)

    def scatter_end(j):
        def each(first, carry):
            block = partial(chip, j, first)
            rs1(first, j, kept(first)).wait_recv()
            block += rr1[first, j, kept(first)].astype(F32)
            rs2(first, j).wait_recv()
            block += rr2[first, j].astype(F32)
            acc[j, :, side(first)] = block
            for k in range(occ):
                tc[j * occ + k, pl.ds(pl.multiple_of(me * size, size), size), side(first)] = (
                    block[k * size:(k + 1) * size].astype(BF16)
                )
            return carry

        lax.fori_loop(0, 2, each, 0)

    def gather_of(j):
        def view(low, count):
            return tc.at[j * occ:(j + 1) * occ, pl.ds(low, count), :]

        return Gather(view, lambda low, count: view(pl.multiple_of(me * size + low, 16), count), size, ag_s.at[j], ag_r.at[j])

    gathers = [gather_of(j) for j in range(occ)]

    def bring(dist, own=False):
        if own:
            copy = pltpu.make_async_copy(slabs_ref, cp.at[z], local.at[0])
            copy.start()
            copy.wait()
            return
        for way in (0, 1):
            @pl.when(amps.exists(way, dist))
            def _():
                def step(k, carry):
                    amps.arrive(way, dist, k)
                    return carry

                lax.fori_loop(0, occ, step, 0)
                origin = amps.origin(way, dist)
                copy = pltpu.make_async_copy(tr_ref.at[origin], cp.at[origin], local.at[0])
                copy.start()
                copy.wait()

    def add_r(origin, j):
        right = tc[pl.ds(j * occ, occ), pl.ds(pl.multiple_of(origin * wide, wide), wide), :].reshape(occ * wide, wide)
        for i in range(occ):
            left = jnp.concatenate([cp[origin, slot[i * occ + k]] for k in range(occ)], axis=1)
            acc[j, i * size:(i + 1) * size] += times(left, right)

    def product(low, high, first, last):
        def each(event, carry):
            dist, way = (event + 1) // 2, lax.rem(event + 1, 2)
            origin = chols.origin(way, dist)

            @pl.when(chols.exists(way, dist))
            def _():
                def step(n, inside):
                    add_r(origin, first + n)
                    return inside

                lax.fori_loop(0, last - first, step, 0)

            return carry

        lax.fori_loop(low, high, each, 0)

    far_chip = 2 * (1 - ybit) + (1 - xbit)
    late_tile = jnp.where(inner, CHAIN, far_tile)

    def product_where(j, near, soon):
        def each(o, carry):
            fits = (o != far_chip) if near else (o == far_chip)
            if soon is not None:
                fits = jnp.logical_and(fits, (o != late_tile) if soon else (o == late_tile))

            @pl.when(fits)
            def _():
                add_r(o, j)

            return carry

        lax.fori_loop(0, CHAIN, each, 0)

    def hand_out(j, i):
        rows = pl.ds(i * size, size)
        return pltpu.make_async_copy(acc.at[j, rows], r_ref.at[j, rows], outs.at[j, i])

    def add_far(j):
        start = far_chip * wide
        near_rows = pl.ds(pl.multiple_of(start + core * size, size), size)
        sib_rows = pl.ds(pl.multiple_of(start + (1 - core) * size, size), size)

        def part(i, rows, which):
            right = tc[j * occ:(j + 1) * occ, rows, :].reshape(tall, wide)
            columns = pl.ds(pl.multiple_of(which * size, size), size)
            left = jnp.concatenate([cp[far_chip, slot[i * occ + k], :, columns] for k in range(occ)], axis=1)
            acc[j, i * size:(i + 1) * size] += times(left, right)

        for i in range(occ):
            part(i, near_rows, core)
        gathers[j].distant()
        for i in range(occ):
            part(i, sib_rows, 1 - core)
            hand_out(j, i).start()

    scatter_one(0)
    scatter_one(1)
    scatter_two(0)
    scatter_one(2)
    scatter_two(1)
    scatter_end(0)
    gathers[0].begin()
    chols.sent(1 - centre)

    @pl.when(inner)
    def _():
        amps.begin(1 - centre)

    scatter_two(2)
    scatter_end(1)
    gathers[1].begin()
    bring(0, own=True)
    gathers[0].relay()
    scatter_end(2)
    gathers[2].begin()
    bring(1)
    gathers[1].relay()
    gathers[0].last()
    gathers[0].near()
    gathers[0].distant()
    product(0, 3, 0, 1)
    bring(2)
    product(3, 5, 0, 1)
    gathers[1].near()
    product_where(1, True, True)
    gathers[1].last()
    gathers[2].relay()
    gathers[1].distant()
    gathers[2].near()
    product_where(2, True, True)
    bring(3)
    product(5, 7, 0, 1)
    product_where(1, True, False)
    product_where(1, False, None)
    for i in range(occ):
        hand_out(0, i).start()
        hand_out(1, i).start()
    gathers[2].last()
    product_where(2, True, False)
    add_far(2)
    for j in range(occ):
        gathers[j].sent()
    for first in (0, 1):
        for j in (1, 2):
            for n in (0, 1):
                rs1(first, j, n).wait_send()
            rs2(first, j).wait_send()

    def y_done(j, carry):
        for first in (0, 1):
            y_copy(j, first).wait_send()
        return carry

    lax.fori_loop(0, occ, y_done, 0)
    amps.sent(0)
    amps.sent(1)
    for j in range(occ):
        for i in range(occ):
            hand_out(j, i).wait()


def in_one_kernel(chol, amps, pairs):
    occ, depth, wide = chol.shape
    _, size, _ = amps.shape
    tall, full = occ * size, size * PLANE
    half = wide // 2
    dma = pltpu.SemaphoreType.DMA
    result, _ = pl.pallas_call(
        whole_kernel,
        out_shape=(
            jax.ShapeDtypeStruct((occ, tall, wide), F32),
            jax.ShapeDtypeStruct((CHAIN, occ * occ, size, wide), BF16),
        ),
        in_specs=[pl.BlockSpec(memory_space=pltpu.SMEM)] + [pl.BlockSpec(memory_space=pl.ANY)] * 2,
        out_specs=(pl.BlockSpec(memory_space=pl.ANY), pl.BlockSpec(memory_space=pl.ANY)),
        scratch_shapes=[
            pltpu.SMEM((occ * occ,), jnp.int32),
            pltpu.VMEM((CHAIN, occ * occ, size, wide), BF16),
            pltpu.VMEM((occ * occ, full, wide), BF16),
            pltpu.VMEM((CHAIN, tall, 2 * depth), BF16),
            pltpu.VMEM((occ, size, depth), BF16),
            pltpu.VMEM((occ, 2 * depth, wide), BF16),
            pltpu.VMEM((occ, tall, wide), F32),
            pltpu.VMEM((2, 2, 2, tall, half), BF16),
            pltpu.VMEM((2, occ, 2, tall, half), BF16),
            pltpu.VMEM((2, 2, tall, half), BF16),
            pltpu.VMEM((2, occ, tall, half), BF16),
            dma((2,)),
            dma((occ, occ)),
            dma((2, CHAIN - 1, occ)),
            dma((2, CHAIN - 1, occ)),
            dma((2, CHAIN - 1, occ)),
            dma((2, CHAIN - 1, occ)),
            dma((occ + 1, PIECES)),
            dma((occ + 1, PIECES)),
            dma((occ,)),
            dma((CHAIN, occ)),
            dma((occ, 2)),
            dma((occ, 2)),
            dma((2, occ, 2)),
            dma((2, occ, 2)),
            dma((2, occ)),
            dma((2, occ)),
        ],
        compiler_params=pltpu.CompilerParams(
            collective_id=0, has_side_effects=True, vmem_limit_bytes=62 * 1024 * 1024
        ),
        cost_estimate=pl.CostEstimate(
            flops=6 * occ * depth * occ * full * wide, bytes_accessed=32 * chol.size, transcendentals=0
        ),
        name="whole",
    )(pairs.T, chol.reshape(amps.shape), amps)
    return result.reshape(occ * occ, size, wide)


def in_steps(chol, amps, pairs):
    occ, depth, _ = chol.shape
    _, size, wide = amps.shape
    order = jnp.arange(occ * occ, dtype=jnp.int32)
    flat_pair = pairs[:, 0] * occ + pairs[:, 1]
    matches = (flat_pair[None, :] == order[:, None]).astype(jnp.int32)
    grid = jnp.take(amps, jnp.sum(matches * order[None, :], axis=1), axis=0, mode="clip")
    slabs = grid.reshape(occ, occ, size, wide)
    cols = lax.all_gather(slabs, "row", axis=2, tiled=True)
    chol_rows = lax.all_gather(chol, "col", axis=2, tiled=True)
    y = lax.dot_general(chol_rows, cols, (((0, 2), (0, 2)), ((), ())), preferred_element_type=F32)
    y = (y + jnp.transpose(chol, (1, 0, 2)).astype(F32)).astype(BF16)
    swapped = lax.all_to_all(chol_rows, "row", split_axis=2, concat_axis=1, tiled=True)
    y = lax.all_gather(y.reshape(depth, occ * wide), "row", axis=0, tiled=True)
    dressed = lax.dot_general(swapped, y, (((1,), (0,)), ((), ())), preferred_element_type=F32)
    dressed_cols = lax.all_gather(dressed.astype(BF16), "row", axis=1, tiled=True)
    rows = lax.all_gather(slabs, "col", axis=3, tiled=True)
    total = lax.dot_general(rows, dressed_cols, (((1, 3), (0, 1)), ((), ())), preferred_element_type=F32)
    total = (total + dressed).reshape(occ, size, occ, wide)
    return jnp.transpose(total, (2, 0, 1, 3)).reshape(occ * occ, size, wide)


def close_kernel(pairs_ref, levels_ref, vir_ref, r_ref, amp_ref, out_ref, base, r, amp, out, r_sem, amp_sem, out_sem):
    size, wide = base.shape
    occ = levels_ref.shape[0]
    slabs = r.shape[0]

    def load(s):
        index = pairs_ref[1, s] * occ + pairs_ref[0, s]
        return (
            pltpu.make_async_copy(r_ref.at[index], r.at[s], r_sem.at[s]),
            pltpu.make_async_copy(amp_ref.at[s], amp.at[s], amp_sem.at[s]),
        )

    def store(s):
        return pltpu.make_async_copy(out.at[s], out_ref.at[s], out_sem.at[s])

    for s in range(AHEAD):
        for copy in load(s):
            copy.start()
    rows = vir_ref[:, pl.ds(pl.multiple_of(lax.axis_index("row") * size, size), size)]
    cols = vir_ref[:, pl.ds(pl.multiple_of(lax.axis_index("col") * wide, wide), wide)]
    rows = jnp.transpose(jnp.broadcast_to(rows, (128, size)), (1, 0))
    base[...] = rows[:, :1] + cols

    def one(s, carry):
        @pl.when(s + AHEAD < slabs)
        def _():
            for copy in load(s + AHEAD):
                copy.start()

        for copy in load(s):
            copy.wait()
        levels = levels_ref[pairs_ref[0, s]] + levels_ref[pairs_ref[1, s]]
        out[s] = r[s] + (base[...] - levels) * amp[s].astype(F32)
        store(s).start()
        return carry

    lax.fori_loop(0, slabs, one, 0)
    for s in range(slabs):
        store(s).wait()


def close(product, amps, eps_occ, eps_vir, pairs):
    slabs, size, wide = amps.shape
    return pl.pallas_call(
        close_kernel,
        out_shape=jax.ShapeDtypeStruct(amps.shape, F32),
        in_specs=[
            pl.BlockSpec(memory_space=pltpu.SMEM),
            pl.BlockSpec(memory_space=pltpu.SMEM),
            pl.BlockSpec(memory_space=pltpu.VMEM),
            pl.BlockSpec(memory_space=pl.ANY),
            pl.BlockSpec(memory_space=pl.ANY),
        ],
        out_specs=pl.BlockSpec(memory_space=pl.ANY),
        scratch_shapes=[
            pltpu.VMEM((size, wide), F32),
            pltpu.VMEM(amps.shape, F32),
            pltpu.VMEM(amps.shape, BF16),
            pltpu.VMEM(amps.shape, F32),
            pltpu.SemaphoreType.DMA((slabs,)),
            pltpu.SemaphoreType.DMA((slabs,)),
            pltpu.SemaphoreType.DMA((slabs,)),
        ],
        compiler_params=pltpu.CompilerParams(vmem_limit_bytes=62 * 1024 * 1024),
        name="close",
    )(pairs.T, eps_occ, eps_vir.reshape(1, -1), product, amps)


def per_device(chol, amps, eps_occ, eps_vir, pairs):
    occ, depth, wide = chol.shape
    size = amps.shape[1]
    one = lax.axis_size("row") == PLANE and lax.axis_size("col") == CHAIN
    one = one and depth == occ * size and wide == 2 * size
    product = (in_one_kernel if one else in_steps)(chol, amps, pairs)
    return close(product, amps, eps_occ, eps_vir, pairs)


def solution(mesh):
    placed = (P(None, "row", "col"), P(None, "row", "col"), P(), P(), P())
    return jax.shard_map(
        per_device, mesh=mesh, in_specs=placed, out_specs=P(None, "row", "col"), check_vma=False
    )
```
